512 devices in a mesh: lvl: 8 (over y_hi, x), row: 64 (over z, y_lo, core).
Axes of the slice: x: 4, y: 8 (y_hi: 2, y_lo: 4; y = y_hi * 4 + y_lo), z: 8, core: 2. Of those that a mesh axis runs over, the one named last changes fastest.
Arguments:
- rhs: float32 [8, 64, 3, 128, 128], P('lvl', 'row'), may hold values from -6 to 6
- op_tiles: float32 [8, 64, 3, 7, 128, 128], P('lvl', 'row'), may hold values from -1 to 4
- op_cols: int32 [8, 64, 3, 7], P('lvl', 'row'), may hold values from 0 to 8, as said below
- link_tiles: float32 [8, 64, 3, 2, 128, 128], P('lvl', 'row'), may hold values from -0.3125 to 0.3125
- level_links: int32 [8, 64, 3, 2], P('lvl', 'row'), may hold values from 0 to 3, as said below
Outputs:
- levels: float32 [8, 64, 3, 128, 128], P('lvl', 'row')
The draws below stay inside these ranges and needn't reach their ends.
Inputs may be any that keep to these rules, and one draw needn't show every extreme that they name: `op_cols`: tile 0 of each block row has code 3 + s (the block itself). Fine blocks have 7 distinct codes; every other block names only codes s, 3 + s, 6 + s of its own slot s. `level_links`: entries of blocks that are not fine are 0.
All inputs are finite; a program needn't handle non-finite values.
Results may differ from the reference program's by a relative error of at most 0.00021.
Values sent between devices are 32-bit elements; how exact they have to be, the bound alone decides.
A program may use at most 64 MiB of HBM per device.

```python
import math
import jax
import jax.numpy as jnp
from jax import lax

BLK = 128
NRHS = 128
SLOTS = 3
OPT = 7
CYCLES = 2
LFINE = 5
LMID = 2
N_LVL = 8
N_ROW = 64


def draw_op_tiles(key, part):
    shape = (N_LVL, N_ROW, SLOTS, OPT, BLK, BLK)
    noise = jax.random.normal(key, shape, jnp.float32)
    first = jnp.where(jnp.arange(OPT) == 0, 1.0, 0.0).astype(jnp.float32)
    eye = jnp.eye(BLK, dtype=jnp.float32)
    return noise * (0.2 / math.sqrt(BLK)) + 2.5 * first[:, None, None] * eye


def draw_op_cols(key, part):
    lvl_ids = jnp.arange(N_LVL)[:, None, None, None]
    slot_ids = jnp.arange(SLOTS)[None, None, :, None]
    count = N_LVL * N_ROW * SLOTS
    keys = jax.random.split(jax.random.fold_in(key, 11), count)
    orders = jax.vmap(lambda one: jax.random.permutation(one, 3 * SLOTS - 1))(keys)
    orders = orders.reshape((N_LVL, N_ROW, SLOTS, 3 * SLOTS - 1))[..., :OPT - 1]
    own = SLOTS + slot_ids
    fine_rest = (own + 1 + orders) % (3 * SLOTS)
    steps = jax.random.randint(jax.random.fold_in(key, 12), (N_LVL, N_ROW, SLOTS, OPT - 1), 0, 3)
    drawn_rest = steps * SLOTS + slot_ids
    rest = jnp.where(lvl_ids < LFINE, fine_rest, drawn_rest)
    own_full = jnp.broadcast_to(own, (N_LVL, N_ROW, SLOTS, 1))
    return jnp.concatenate([own_full, rest], axis=3).astype(jnp.int32)


def draw_level_links(key, part):
    lvl_ids = jnp.arange(N_LVL)[:, None, None, None]
    picks = jax.random.randint(jax.random.fold_in(key, 21), (N_LVL, N_ROW, SLOTS, 2), 0, 2 * LMID)
    return jnp.where(lvl_ids < LFINE, picks, 0).astype(jnp.int32)


def block_scale(own_key, shape, shards, low, high):
    factor_of, own = 1.0, jax.random.fold_in(own_key, 6)
    for position, parts in shards:
        draws = jnp.exp(jax.random.uniform(jax.random.fold_in(own, position), (parts,), jnp.float32, low / len(shards), high / len(shards)))
        factor_of = factor_of * jnp.repeat(draws, shape[position] // parts).reshape([-1 if axis == position else 1 for axis in range(len(shape))])
    return factor_of


def gaussian(rng, shape, deviation, bound, cuts=(), kind=jnp.bfloat16):
    drawn = jax.random.normal(rng, shape, jnp.float32) * deviation
    if len(cuts) > 0:
        drawn = block_scale(rng, shape, cuts, -0.22, 0.18) * drawn
    return jnp.clip(drawn, min=-bound, max=bound).astype(kind)


def setup_inputs(seed: int = 0) -> dict:
    seeds = jax.random.split(jax.random.key(seed), 6)
    return {
        "rhs": gaussian(seeds[0], (N_LVL, N_ROW, SLOTS, BLK, NRHS), 1.0, 6.0, ((0, 8), (1, 64)), jnp.float32),
        "op_tiles": draw_op_tiles(jax.random.fold_in(seeds[5], 71), 0),
        "op_cols": draw_op_cols(jax.random.fold_in(seeds[5], 71), 0),
        "link_tiles": gaussian(seeds[3], (N_LVL, N_ROW, SLOTS, 2, BLK, BLK), (BLK * SLOTS) ** -0.5, 0.3125, ((0, 8), (1, 64)), jnp.float32),
        "level_links": draw_level_links(jax.random.fold_in(seeds[5], 71), 0),
    }


HIGH = lax.Precision.HIGHEST
COEF_ZERO = 0.9
COEF_ONE = -0.36
COEF_TWO = 0.05


def level_masks():
    lvl_ids = jnp.arange(N_LVL)[:, None]
    slot_ids = jnp.arange(SLOTS)[None, :]
    fine = jnp.where((lvl_ids < LFINE) & (slot_ids >= 0), 1.0, 0.0).astype(jnp.float32)
    mid_slot = (slot_ids == 0) | (slot_ids == 2)
    mid = jnp.where((lvl_ids >= LFINE) & (lvl_ids < LFINE + LMID) & mid_slot, 1.0, 0.0).astype(jnp.float32)
    coarse = jnp.where((lvl_ids == N_LVL - 1) & (slot_ids == 1), 1.0, 0.0).astype(jnp.float32)
    return fine, mid, coarse


def spread(mask):
    return mask[:, None, :, None, None]


def take_mid(field):
    sub = field[LFINE:LFINE + LMID][:, :, 0:3:2]
    sub = jnp.moveaxis(sub, 2, 1)
    return sub.reshape((2 * LMID,) + sub.shape[2:])


def put_mid(field, values):
    values = values.reshape((LMID, 2) + values.shape[1:])
    values = jnp.moveaxis(values, 1, 2)
    field = field.at[LFINE:LFINE + LMID, :, 0].set(values[:, :, 0])
    return field.at[LFINE:LFINE + LMID, :, 2].set(values[:, :, 1])


def apply_operator(field, op_tiles, op_cols, keep):
    edge = jnp.zeros_like(field[:, :1])
    padded = jnp.concatenate([edge, field, edge], axis=1)

    def one_level(items):
        pad_level, tiles_level, cols_level = items
        candidates = jnp.stack([pad_level[:-2], pad_level[1:-1], pad_level[2:]], axis=1)
        candidates = candidates.reshape((N_ROW, 3 * SLOTS, BLK, NRHS))
        picked = jax.vmap(lambda cand, cols: cand[cols])(candidates, cols_level)
        return jnp.einsum("rsjab,rsjbn->rsan", tiles_level, picked, precision=HIGH)

    image = lax.map(one_level, (padded, op_tiles, op_cols))
    return image * spread(keep)


def reference(rhs, op_tiles, op_cols, link_tiles, level_links):
    fine, mid, coarse = level_masks()
    keep = fine + mid + coarse
    mid_ids = jnp.arange(2 * LMID)
    to_mid = (level_links[..., 0][..., None] == mid_ids).astype(jnp.float32) * fine[:, None, :, None]
    from_mid = (level_links[..., 1][..., None] == mid_ids).astype(jnp.float32) * fine[:, None, :, None]
    restrict = link_tiles[:, :, :, 0]
    prolong = link_tiles[:, :, :, 1]
    mid_restrict = take_mid(restrict)
    mid_prolong = take_mid(prolong)
    solution = jnp.zeros_like(rhs)
    mid_fix = jnp.zeros((2 * LMID, N_ROW, BLK, NRHS), jnp.float32)
    coarse_fix = jnp.zeros((N_ROW, BLK, NRHS), jnp.float32)
    for cycle in range(CYCLES):
        if cycle == 0:
            resid = rhs * spread(fine)
        else:
            resid = (rhs - apply_operator(solution, op_tiles, op_cols, keep)) * spread(fine)
        terms = jnp.einsum("lrsab,lrsbn->lrsan", restrict, resid, precision=HIGH)
        mid_resid = jnp.einsum("lrsk,lrsan->kran", to_mid, terms, precision=HIGH)
        fine_sum = jnp.sum(terms * spread(fine), axis=(0, 2))
        coarse_resid = jnp.einsum("krab,krbn->ran", mid_restrict, mid_resid, precision=HIGH) + 0.5 * fine_sum
        level_resid = put_mid(resid, mid_resid)
        level_resid = level_resid.at[N_LVL - 1, :, 1].set(coarse_resid)
        first = apply_operator(level_resid, op_tiles, op_cols, keep)
        second = apply_operator(first, op_tiles, op_cols, keep)
        smooth = COEF_ZERO * level_resid + COEF_ONE * first + COEF_TWO * second
        coarse_fix = smooth[N_LVL - 1, :, 1]
        mid_fix = take_mid(smooth) + jnp.einsum("krab,rbn->kran", mid_prolong, coarse_fix, precision=HIGH)
        chosen = jnp.einsum("lrsk,kran->lrsan", from_mid, mid_fix, precision=HIGH)
        chosen = chosen + coarse_fix[None, :, None]
        fine_fix = smooth + jnp.einsum("lrsab,lrsbn->lrsan", prolong, chosen, precision=HIGH)
        solution = solution + fine_fix * spread(fine)
    levels = put_mid(solution, mid_fix)
    levels = levels.at[N_LVL - 1, :, 1].set(coarse_fix)
    return levels
```

```python
import jax
import jax.numpy as jnp
from jax import lax
from jax.experimental import pallas as pl
from jax.experimental.pallas import tpu as pltpu
from jax.sharding import PartitionSpec as P

CYCLES = 2
B = 128
SLOTS = 3
OPT = 7
COEF_ZERO = 0.9
COEF_ONE = -0.36
COEF_TWO = 0.05
MESH = pl.DeviceIdType.MESH
F32 = jnp.float32
BF16 = jnp.bfloat16


def halves(value):
    high = value.astype(BF16)
    return high, (value - high.astype(F32)).astype(BF16)


def stacked(value):
    return jnp.concatenate(halves(value), axis=0)


def beside(value):
    return jnp.concatenate(halves(value), axis=1)


def product(left, right):
    full = jnp.dot(left, right, preferred_element_type=F32)
    rows, columns = full.shape[0] // 2, full.shape[1] // 2
    cross = full[:rows, columns:] + full[rows:, :columns]
    return full[:rows, :columns] + (cross + full[rows:, columns:])


def kernel(
    n_row,
    rhs_hbm, ops_hbm, cols, links_hbm, targets, out,
    rhs, ops, links, wide, small, link_parts,
    field, halo, rs_src, rs_in, sum_src, mid_in, part_src, coarse_in, fix, fbuf,
    sol, smooth,
    in_sem, halo_send, halo_recv, rs_send, rs_recv, sum_send, mid_recv, four_send,
    part_send, coarse_recv, fix_send, fix_recv, f_send, gather_send, f_recv,
):
    lvl = lax.axis_index("lvl")
    row = lax.axis_index("row")
    is_fine = lvl < 5
    is_mid = (lvl >= 5) & (lvl < 7)
    is_coarse = lvl == 7
    has = (row > 0, row < n_row - 1)
    near = (row - 1, row + 1)

    loads = [
        pltpu.make_async_copy(rhs_hbm, rhs, in_sem.at[0]),
        pltpu.make_async_copy(links_hbm, links, in_sem.at[1]),
        pltpu.make_async_copy(ops_hbm, ops, in_sem.at[2]),
    ]
    for load in loads:
        load.start()

    barrier = pltpu.get_barrier_semaphore()
    for step in range(1, 8):
        pl.semaphore_signal(
            barrier, inc=1, device_id={"lvl": lax.rem(lvl + step, 8), "row": row}, device_id_type=MESH
        )
    for side in range(2):
        @pl.when(has[side])
        def _():
            pl.semaphore_signal(
                barrier, inc=1, device_id={"lvl": lvl, "row": near[side]}, device_id_type=MESH
            )

    def meet():
        pl.semaphore_wait(barrier, 7 + sum(one.astype(jnp.int32) for one in has))

    def copy(src, dst, send, recv, to_lvl, to_row=None):
        return pltpu.make_async_remote_copy(
            src_ref=src, dst_ref=dst, send_sem=send, recv_sem=recv,
            device_id={"lvl": to_lvl, "row": row if to_row is None else to_row},
            device_id_type=MESH,
        )

    def halo_copy(turn, side, src, rows):
        other = 1 - side
        return copy(
            src.at[pl.ds(0, rows)], halo.at[turn, other, pl.ds(0, rows)],
            halo_send.at[turn, side], halo_recv.at[turn, other], lvl, near[side],
        )

    def halo_start(turn, src, rows):
        for side in range(2):
            @pl.when(has[side])
            def _():
                halo_copy(turn, side, src, rows).start()

    def halo_sent(turn, src, rows):
        for side in range(2):
            @pl.when(has[side])
            def _():
                halo_copy(turn, side, src, rows).wait_send()

    def halo_arrived(turn, side, rows):
        pltpu.make_async_copy(
            halo.at[turn, side, pl.ds(0, rows)], halo.at[turn, side, pl.ds(0, rows)],
            halo_recv.at[turn, side],
        ).wait()

    def arrived(ref, sem):
        pltpu.make_async_copy(ref, ref, sem).wait()

    def split_links():
        loads[1].wait()
        for s in range(SLOTS):
            for kind in range(2):
                link_parts[s, kind] = stacked(links[s, kind])

    def code_of(s, j):
        return cols[s * OPT + j]

    def gathered_tile(s, code):
        total = jnp.zeros((B, B), F32)
        for j in range(OPT):
            total = total + jnp.where(code_of(s, j) == code, F32(1), F32(0)) * ops[s * OPT + j]
        return total

    @pl.when(is_fine)
    def _():
        split_links()
        loads[0].wait()

        def restrict(cycle, resid_of):
            terms = [
                product(link_parts[s, 0], beside(resid_of(s))) for s in range(SLOTS)
            ]
            for k in range(4):
                total = jnp.zeros((B, B), F32)
                for s in range(SLOTS):
                    hit = jnp.where(targets[s * 2] == k, F32(1), F32(0))
                    total = total + hit * terms[s]
                rs_src[cycle, k] = total

        def rs_copy(cycle, step):
            to = lax.rem(lvl + step, 4)
            return copy(
                rs_src.at[cycle, to], rs_in.at[cycle, lvl],
                rs_send.at[cycle, step], rs_recv.at[cycle, lvl], to,
            )

        def sum_copy(cycle):
            return copy(
                sum_src.at[cycle], mid_in.at[cycle, lax.rem(lvl, 2), 0],
                sum_send.at[cycle], mid_recv.at[cycle, lax.rem(lvl, 2), 0], 5 + lvl // 2,
            )

        def four_copy(cycle, k):
            return copy(
                rs_src.at[cycle, k], mid_in.at[cycle, k % 2, 1],
                four_send.at[cycle, k], mid_recv.at[cycle, k % 2, 1], 5 + k // 2,
            )

        def gather_copy(cycle, step):
            return copy(
                fbuf.at[cycle, lvl], fbuf.at[cycle, lvl],
                gather_send.at[cycle, step], f_recv.at[cycle, lvl], lax.rem(lvl + step, 4),
            )

        def send_terms(cycle):
            @pl.when(lvl < 4)
            def _():
                for step in range(1, 4):
                    rs_copy(cycle, step).start()

            @pl.when(lvl == 4)
            def _():
                for k in range(4):
                    four_copy(cycle, k).start()

        def send_sum(cycle):
            @pl.when(lvl < 4)
            def _():
                total = rs_src[cycle, lvl]
                for step in range(1, 4):
                    source = lax.rem(lvl + step, 4)
                    arrived(rs_in.at[cycle, source], rs_recv.at[cycle, source])
                    total = total + rs_in[cycle, source]
                sum_src[cycle] = total
                sum_copy(cycle).start()

        def collect(cycle):
            @pl.when(lvl < 4)
            def _():
                arrived(fbuf.at[cycle, lvl], f_recv.at[cycle, lvl])
                for step in range(1, 4):
                    gather_copy(cycle, step).start()
                for step in range(1, 4):
                    source = lax.rem(lvl + step, 4)
                    arrived(fbuf.at[cycle, source], f_recv.at[cycle, source])

            @pl.when(lvl == 4)
            def _():
                for k in range(4):
                    arrived(fbuf.at[cycle, k], f_recv.at[cycle, k])

        def image(turn, src, dst):
            dst[...] = product(wide[1], beside(src[...]))
            for side in range(2):
                @pl.when(has[side])
                def _():
                    halo_arrived(turn, side, SLOTS * B)
                    dst[...] = dst[...] + product(wide[2 * side], beside(halo[turn, side]))

        restrict(0, lambda s: rhs[pl.ds(s * B, B)])
        meet()
        send_terms(0)
        halo_start(0, rhs, SLOTS * B)

        loads[2].wait()

        def dense(s, carry):
            for code in range(3 * SLOTS):
                high, low = halves(gathered_tile(s, code))
                columns = pl.ds((code % SLOTS) * B, B)
                wide[code // SLOTS, pl.ds(pl.multiple_of(s * B, B), B), columns] = high
                wide[code // SLOTS, pl.ds(pl.multiple_of((SLOTS + s) * B, B), B), columns] = low
            return carry

        lax.fori_loop(0, SLOTS, dense, 0)

        sent = []
        for cycle in range(CYCLES):
            if cycle == 0:
                base = 0
                resid = rhs
                sent.append((0, rhs))
            else:
                base = 3
                halo_start(2, sol, SLOTS * B)
                image(2, sol, smooth)
                resid = field.at[3]
                resid[...] = rhs[...] - smooth[...]
                restrict(1, lambda s: field[3, pl.ds(s * B, B)])
                send_terms(1)
                halo_start(3, resid, SLOTS * B)
                sent.append((2, sol))
                sent.append((3, resid))
            send_sum(cycle)
            first = field.at[base + 1]
            image(base, resid, first)

            @pl.when(lvl < 4)
            def _():
                sum_copy(cycle).wait_send()

            halo_start(base + 1, first, SLOTS * B)
            sent.append((base + 1, first))
            image(base + 1, first, smooth)
            smooth[...] = COEF_ZERO * resid[...] + COEF_ONE * first[...] + COEF_TWO * smooth[...]
            if cycle == 1:
                smooth[...] = sol[...] + smooth[...]
            collect(cycle)
            dest = sol if cycle == 0 else out
            for s in range(SLOTS):
                chosen = fbuf[cycle, targets[s * 2 + 1]]
                rows = pl.ds(s * B, B)
                dest[rows] = smooth[rows] + product(link_parts[s, 1], beside(chosen))

        for turn, src in sent:
            halo_sent(turn, src, SLOTS * B)
        for cycle in range(CYCLES):
            @pl.when(lvl < 4)
            def _():
                for step in range(1, 4):
                    rs_copy(cycle, step).wait_send()
                    gather_copy(cycle, step).wait_send()

            @pl.when(lvl == 4)
            def _():
                for k in range(4):
                    four_copy(cycle, k).wait_send()

    def narrow(p, s):
        for near_row in range(3):
            small[p, near_row] = stacked(gathered_tile(s, near_row * SLOTS + s))

    def level_image(turn, count, dst):
        rows = count * B
        for p in range(count):
            part = pl.ds(p * B, B)
            dst[part] = product(small[p, 1], beside(field[turn, part]))
        for side in range(2):
            @pl.when(has[side])
            def _():
                halo_arrived(turn, side, rows)
                for p in range(count):
                    part = pl.ds(p * B, B)
                    dst[part] = dst[part] + product(small[p, 2 * side], beside(halo[turn, side, part]))

    def level_smooth(base, count):
        rows = count * B
        first = field.at[base + 1]
        level_image(base, count, first)
        halo_start(base + 1, first, rows)
        level_image(base + 1, count, smooth)
        part = pl.ds(0, rows)
        smooth[part] = (
            COEF_ZERO * field[base, part] + COEF_ONE * first[part] + COEF_TWO * smooth[part]
        )

    @pl.when(is_mid)
    def _():
        pair = lvl - 5
        split_links()
        eye = (
            lax.broadcasted_iota(jnp.int32, (B, B), 0) == lax.broadcasted_iota(jnp.int32, (B, B), 1)
        ).astype(F32)
        for p in range(2):
            link_parts[2 * p, 0] = stacked(links[2 * p, 0] + 0.5 * eye)
        loads[0].wait()
        loads[2].wait()
        for p in range(2):
            narrow(p, 2 * p)
        meet()

        def part_copy(cycle):
            return copy(
                part_src.at[cycle], coarse_in.at[cycle, pair],
                part_send.at[cycle], coarse_recv.at[cycle, pair], 7,
            )

        def f_copy(cycle, p, four):
            k = 2 * pair + p
            return copy(
                fbuf.at[cycle, k], fbuf.at[cycle, k],
                f_send.at[cycle, p, four], f_recv.at[cycle, k], 4 if four else k,
            )

        for cycle in range(CYCLES):
            base = 3 * cycle
            for p in range(2):
                for source in (1, 0):
                    arrived(mid_in.at[cycle, p, source], mid_recv.at[cycle, p, source])
                field[base, pl.ds(p * B, B)] = mid_in[cycle, p, 0] + mid_in[cycle, p, 1]
            total = product(link_parts[0, 0], beside(field[base, pl.ds(0, B)]))
            part_src[cycle] = total + product(link_parts[2, 0], beside(field[base, pl.ds(B, B)]))
            part_copy(cycle).start()
            halo_start(base, field.at[base], 2 * B)
            level_smooth(base, 2)
            arrived(fix.at[cycle], fix_recv.at[cycle])
            coarse = beside(fix[cycle])
            for p in range(2):
                value = smooth[pl.ds(p * B, B)] + product(link_parts[2 * p, 1], coarse)
                smooth[pl.ds(p * B, B)] = value
                fbuf[cycle, 2 * pair + p] = value + fix[cycle]
                for four in range(2):
                    f_copy(cycle, p, four).start()
        out[pl.ds(0, B)] = smooth[pl.ds(0, B)]
        out[pl.ds(B, B)] = jnp.zeros((B, B), F32)
        out[pl.ds(2 * B, B)] = smooth[pl.ds(B, B)]
        for cycle in range(CYCLES):
            part_copy(cycle).wait_send()
            for turn in (3 * cycle, 3 * cycle + 1):
                halo_sent(turn, field.at[turn], 2 * B)
            for p in range(2):
                for four in range(2):
                    f_copy(cycle, p, four).wait_send()

    @pl.when(is_coarse)
    def _():
        loads[0].wait()
        loads[1].wait()
        loads[2].wait()
        narrow(0, 1)
        meet()

        def fix_copy(cycle, pair):
            return copy(
                fix.at[cycle], fix.at[cycle], fix_send.at[cycle, pair], fix_recv.at[cycle], 5 + pair
            )

        for cycle in range(CYCLES):
            base = 3 * cycle
            for pair in range(2):
                arrived(coarse_in.at[cycle, pair], coarse_recv.at[cycle, pair])
            field[base, pl.ds(0, B)] = coarse_in[cycle, 0] + coarse_in[cycle, 1]
            halo_start(base, field.at[base], B)
            level_smooth(base, 1)
            fix[cycle] = smooth[pl.ds(0, B)]
            for pair in range(2):
                fix_copy(cycle, pair).start()
        out[pl.ds(0, B)] = jnp.zeros((B, B), F32)
        out[pl.ds(B, B)] = fix[CYCLES - 1]
        out[pl.ds(2 * B, B)] = jnp.zeros((B, B), F32)
        for cycle in range(CYCLES):
            for turn in (3 * cycle, 3 * cycle + 1):
                halo_sent(turn, field.at[turn], B)
            for pair in range(2):
                fix_copy(cycle, pair).wait_send()


def solution(mesh):
    n_row = mesh.shape["row"]

    def per_device(rhs, op_tiles, op_cols, link_tiles, level_links):
        dma = pltpu.SemaphoreType.DMA
        block = lambda *lead: pltpu.VMEM(lead + (B, B), F32)
        out = pl.pallas_call(
            lambda *refs: kernel(n_row, *refs),
            name="multigrid",
            out_shape=jax.ShapeDtypeStruct((SLOTS * B, B), F32),
            in_specs=[
                pl.BlockSpec(memory_space=pl.ANY),
                pl.BlockSpec(memory_space=pl.ANY),
                pl.BlockSpec(memory_space=pltpu.SMEM),
                pl.BlockSpec(memory_space=pl.ANY),
                pl.BlockSpec(memory_space=pltpu.SMEM),
            ],
            out_specs=pl.BlockSpec(memory_space=pltpu.VMEM),
            scratch_shapes=[
                pltpu.VMEM((SLOTS * B, B), F32),
                block(SLOTS * OPT),
                block(SLOTS, 2),
                pltpu.VMEM((3, 2 * SLOTS * B, SLOTS * B), BF16),
                pltpu.VMEM((2, 3, 2 * B, B), BF16),
                pltpu.VMEM((SLOTS, 2, 2 * B, B), BF16),
                pltpu.VMEM((5, SLOTS * B, B), F32),
                pltpu.VMEM((5, 2, SLOTS * B, B), F32),
                block(CYCLES, 4),
                block(CYCLES, 4),
                block(CYCLES),
                block(CYCLES, 2, 2),
                block(CYCLES),
                block(CYCLES, 2),
                block(CYCLES),
                block(CYCLES, 4),
                pltpu.VMEM((SLOTS * B, B), F32),
                pltpu.VMEM((SLOTS * B, B), F32),
                dma((3,)),
                dma((5, 2)),
                dma((5, 2)),
                dma((CYCLES, 4)),
                dma((CYCLES, 4)),
                dma((CYCLES,)),
                dma((CYCLES, 2, 2)),
                dma((CYCLES, 4)),
                dma((CYCLES,)),
                dma((CYCLES, 2)),
                dma((CYCLES, 2)),
                dma((CYCLES,)),
                dma((CYCLES, 2, 2)),
                dma((CYCLES, 4)),
                dma((CYCLES, 4)),
            ],
            compiler_params=pltpu.CompilerParams(
                collective_id=0, has_side_effects=True, vmem_limit_bytes=60 * 1024 * 1024
            ),
        )(
            rhs.reshape(SLOTS * B, B),
            op_tiles.reshape(SLOTS * OPT, B, B),
            op_cols.reshape(SLOTS * OPT),
            link_tiles.reshape(SLOTS, 2, B, B),
            level_links.reshape(SLOTS * 2),
        )
        return out.reshape(1, 1, SLOTS, B, B)

    placed = (
        P("lvl", "row", None, None, None),
        P("lvl", "row", None, None, None, None),
        P("lvl", "row", None, None),
        P("lvl", "row", None, None, None, None),
        P("lvl", "row", None, None),
    )
    return jax.shard_map(
        per_device,
        mesh=mesh,
        in_specs=placed,
        out_specs=P("lvl", "row", None, None, None),
        check_vma=False,
    )
```

```python
import functools
import types

import jax
import jax.numpy as jnp
from jax import lax
from jax.experimental import pallas as pl
from jax.experimental.pallas import tpu as pltpu
from jax.sharding import PartitionSpec as P

B = 128
SLOTS = 3
OPT = 7
COEF_ZERO = 0.9
COEF_ONE = -0.36
COEF_TWO = 0.05
MESH = pl.DeviceIdType.MESH
F32 = jnp.float32
BF16 = jnp.bfloat16


def halves(value):
    high = value.astype(BF16)
    return high, (value - high.astype(F32)).astype(BF16)


def stacked(value):
    return jnp.concatenate(halves(value), axis=0)


def beside(value):
    return jnp.concatenate(halves(value), axis=1)


def product(left, right):
    full = jnp.dot(left, right, preferred_element_type=F32)
    rows, columns = full.shape[0] // 2, full.shape[1] // 2
    cross = full[:rows, columns:] + full[rows:, :columns]
    return full[:rows, :columns] + (cross + full[rows:, columns:])


def kernel(n_row, names, rhs_hbm, ops_hbm, cols, links_hbm, targets, out, *refs):
    m = types.SimpleNamespace(**dict(zip(names, refs)))
    lvl = lax.axis_index("lvl")
    row = lax.axis_index("row")
    is_fine = lvl < 5
    is_mid = (lvl >= 5) & (lvl < 7)
    is_coarse = lvl == 7
    plane = lvl < 4
    four = lvl == 4
    root = lvl == 0
    has = (row > 0, row < n_row - 1)
    near = (row - 1, row + 1)
    far = (-2, -1, 1, 2)
    has_far = (row > 1, row > 0, row < n_row - 1, row < n_row - 2)

    load_rhs = pltpu.make_async_copy(rhs_hbm, m.rhs, m.in_sem.at[0])
    load_links = pltpu.make_async_copy(links_hbm, m.links, m.in_sem.at[1])
    load_ops = pltpu.make_async_copy(ops_hbm, m.ops, m.in_sem.at[2])
    for load in (load_rhs, load_links, load_ops):
        load.start()

    barrier = pltpu.get_barrier_semaphore()
    for step in range(1, 8):
        pl.semaphore_signal(
            barrier, inc=1, device_id={"lvl": lax.rem(lvl + step, 8), "row": row}, device_id_type=MESH
        )
    for step, there in zip(far, has_far):
        @pl.when(there)
        def _():
            pl.semaphore_signal(
                barrier, inc=1, device_id={"lvl": lvl, "row": row + step}, device_id_type=MESH
            )

    def meet():
        pl.semaphore_wait(barrier, 7 + sum(one.astype(jnp.int32) for one in has_far))

    pending = []

    def go(make, cond=None):
        pending.append((make, cond))
        if cond is None:
            make().start()
        else:
            pl.when(cond)(lambda: make().start())

    def drain():
        for make, cond in pending:
            if cond is None:
                make().wait_send()
            else:
                pl.when(cond)(lambda: make().wait_send())
        pending.clear()

    def copy(src, dst, send, recv, to_lvl, to_row=None):
        return pltpu.make_async_remote_copy(
            src_ref=src, dst_ref=dst, send_sem=send, recv_sem=recv,
            device_id={"lvl": to_lvl, "row": row if to_row is None else to_row},
            device_id_type=MESH,
        )

    def arrived(ref, sem):
        pltpu.make_async_copy(ref, ref, sem).wait()

    def halo_go(turn, src, rows):
        part = pl.ds(0, rows)
        for side in range(2):
            go(
                lambda side=side: copy(
                    src.at[part], m.halo.at[turn, 1 - side, part],
                    m.halo_send.at[turn, side], m.halo_recv.at[turn, 1 - side], lvl, near[side],
                ),
                has[side],
            )

    def halo_arrived(turn, side, rows):
        arrived(m.halo.at[turn, side, pl.ds(0, rows)], m.halo_recv.at[turn, side])

    def code_of(s, j):
        return cols[s * OPT + j]

    def gathered_tile(s, code):
        total = jnp.zeros((B, B), F32)
        for j in range(OPT):
            total = total + jnp.where(code_of(s, j) == code, F32(1), F32(0)) * m.ops[s * OPT + j]
        return total

    def clear_missing(ref, conditions):
        for i, there in enumerate(conditions):
            @pl.when(jnp.logical_not(there))
            def _():
                ref[i] = jnp.zeros((B, B), F32)

    def coarse_send(cycle):
        for i in range(4):
            go(
                lambda i=i: copy(
                    m.cv.at[cycle], m.chalo.at[cycle, 3 - i],
                    m.chalo_send.at[cycle, i], m.chalo_recv.at[cycle, 3 - i], lvl, row + far[i],
                ),
                has_far[i] & (is_coarse if cycle == 0 else root),
            )

    def coarse_solve(cycle):
        own = product(m.st_own[...], beside(m.cv[cycle]))
        for i in range(4):
            @pl.when(has_far[i])
            def _():
                arrived(m.chalo.at[cycle, i], m.chalo_recv.at[cycle, i])
        around = beside(m.chalo[cycle].reshape(4 * B, B))
        m.fix[cycle] = own + product(m.st_far[...], around)

    def split_stencil():
        m.st_own[...] = stacked(m.st[2])
        for i, d in enumerate((0, 1, 3, 4)):
            m.st_far[:, pl.ds(i * B, B)] = stacked(m.st[d])

    @pl.when(is_fine)
    def _():
        load_links.wait()
        for s in range(SLOTS):
            for kind in range(2):
                m.link_parts[s, kind] = stacked(m.links[s, kind])
        load_rhs.wait()

        def restrict(cycle, resid_of):
            terms = [
                product(m.link_parts[s, 0], beside(resid_of(s))) for s in range(SLOTS)
            ]
            for k in range(4):
                total = jnp.zeros((B, B), F32)
                for s in range(SLOTS):
                    hit = jnp.where(targets[s * 2] == k, F32(1), F32(0))
                    total = total + hit * terms[s]
                m.rs_src[cycle, k] = total
            return terms

        def send_terms(cycle):
            for step in range(1, 4):
                to = lax.rem(lvl + step, 4)
                go(
                    lambda step=step, to=to: copy(
                        m.rs_src.at[cycle, to], m.rs_in.at[cycle, lvl],
                        m.rs_send.at[cycle, step], m.rs_recv.at[cycle, lvl], to,
                    ),
                    plane,
                )

        def plane_sum(cycle):
            total = m.rs_src[cycle, lvl]
            for step in range(1, 4):
                source = lax.rem(lvl + step, 4)
                arrived(m.rs_in.at[cycle, source], m.rs_recv.at[cycle, source])
                total = total + m.rs_in[cycle, source]
            return total

        def gather_go(cycle):
            for step in range(1, 4):
                go(
                    lambda step=step: copy(
                        m.fbuf.at[cycle, lvl], m.fbuf.at[cycle, lvl],
                        m.gather_send.at[cycle, step], m.f_recv.at[cycle, lvl], lax.rem(lvl + step, 4),
                    ),
                    plane,
                )

        def image(turn, src, dst):
            dst[...] = product(m.wide[1], beside(src[...]))
            for side in range(2):
                @pl.when(has[side])
                def _():
                    halo_arrived(turn, side, SLOTS * B)
                    dst[...] = dst[...] + product(m.wide[2 * side], beside(m.halo[turn, side]))

        def correct(cycle, dest):
            for s in range(SLOTS):
                chosen = m.fbuf[cycle, targets[s * 2 + 1]]
                rows = pl.ds(s * B, B)
                dest[rows] = m.smooth[rows] + product(m.link_parts[s, 1], beside(chosen))

        def blend(resid, first):
            return COEF_ZERO * resid[...] + COEF_ONE * first[...] + COEF_TWO * m.smooth[...]

        restrict(0, lambda s: m.rhs[pl.ds(s * B, B)])
        meet()
        send_terms(0)
        for k in range(4):
            go(
                lambda k=k: copy(
                    m.rs_src.at[0, k], m.mid_in.at[k % 2, 1],
                    m.four_send.at[k], m.mid_recv.at[k % 2, 1], 5 + k // 2,
                ),
                four,
            )
        halo_go(0, m.rhs, SLOTS * B)

        load_ops.wait()

        def dense(s, carry):
            for code in range(3 * SLOTS):
                high, low = halves(gathered_tile(s, code))
                columns = pl.ds((code % SLOTS) * B, B)
                m.wide[code // SLOTS, pl.ds(pl.multiple_of(s * B, B), B), columns] = high
                m.wide[code // SLOTS, pl.ds(pl.multiple_of((SLOTS + s) * B, B), B), columns] = low
            return carry

        lax.fori_loop(0, SLOTS, dense, 0)

        sum_copy = lambda: copy(
            m.sum_src, m.mid_in.at[lax.rem(lvl, 2), 0],
            m.sum_send, m.mid_recv.at[lax.rem(lvl, 2), 0], 5 + lvl // 2,
        )

        @pl.when(plane)
        def _():
            m.sum_src[...] = plane_sum(0)
            sum_copy().start()

        first = m.field.at[1]
        image(0, m.rhs, first)

        @pl.when(plane)
        def _():
            sum_copy().wait_send()

        halo_go(1, first, SLOTS * B)

        @pl.when(plane)
        def _():
            arrived(m.t_buf.at[lvl], m.t_recv.at[lvl])

        for step in range(1, 4):
            go(
                lambda step=step: copy(
                    m.t_buf.at[lvl], m.t_buf.at[lvl],
                    m.t_send.at[step], m.t_recv.at[lvl], lax.rem(lvl + step, 4),
                ),
                plane,
            )
        image(1, first, m.smooth)
        m.smooth[...] = blend(m.rhs, first)

        @pl.when(plane)
        def _():
            arrived(m.p_buf, m.p_recv)
            m.p_part[...] = stacked(m.p_buf[...])
            for step in range(1, 4):
                source = lax.rem(lvl + step, 4)
                arrived(m.t_buf.at[source], m.t_recv.at[source])

        @pl.when(four)
        def _():
            for k in range(4):
                arrived(m.t_buf.at[k], m.t_recv.at[k])

        for k in range(4):
            m.t_part[k] = stacked(m.t_buf[k])

        @pl.when(root)
        def _():
            arrived(m.st, m.st_recv)
            split_stencil()
            clear_missing(m.chalo.at[1], has_far)

        @pl.when(plane)
        def _():
            clear_missing(m.mhalo.at[0], has)
            clear_missing(m.mhalo.at[1], has)
            arrived(m.fbuf.at[0, lvl], m.f_recv.at[0, lvl])

        gather_go(0)

        @pl.when(plane)
        def _():
            for step in range(1, 4):
                source = lax.rem(lvl + step, 4)
                arrived(m.fbuf.at[0, source], m.f_recv.at[0, source])

        @pl.when(four)
        def _():
            for k in range(4):
                arrived(m.fbuf.at[0, k], m.f_recv.at[0, k])

        correct(0, m.sol)

        halo_go(2, m.sol, SLOTS * B)
        image(2, m.sol, m.smooth)
        resid = m.field.at[3]
        resid[...] = m.rhs[...] - m.smooth[...]
        terms = restrict(1, lambda s: m.field[3, pl.ds(s * B, B)])
        send_terms(1)
        for k in range(4):
            go(
                lambda k=k: copy(
                    m.rs_src.at[1, k], m.rs_in.at[1, 4], m.four_send.at[4 + k], m.rs_recv.at[1, 4], k
                ),
                four,
            )
        total = jnp.zeros((B, B), F32)
        for s in range(SLOTS):
            total = total + product(m.t_part[targets[s * 2]], beside(terms[s]))
        m.u_src[...] = total
        slot = jnp.maximum(lvl - 1, 0)
        go(
            lambda: copy(m.u_src, m.u_in.at[slot], m.u_send, m.u_recv.at[slot], 0),
            jnp.logical_not(root),
        )
        halo_go(3, resid, SLOTS * B)

        def mid_halo_go(turn):
            for side in range(2):
                go(
                    lambda side=side: copy(
                        m.mv.at[turn], m.mhalo.at[turn, 1 - side],
                        m.mhalo_send.at[turn, side], m.mhalo_recv.at[turn, 1 - side], lvl, near[side],
                    ),
                    has[side] & plane,
                )

        def mid_image(turn):
            own = product(m.small[0, 1], beside(m.mv[turn]))
            for side in range(2):
                @pl.when(has[side])
                def _():
                    arrived(m.mhalo.at[turn, side], m.mhalo_recv.at[turn, side])
            for side in range(2):
                own = own + product(m.small[0, 2 * side], beside(m.mhalo[turn, side]))
            return own

        @pl.when(plane)
        def _():
            total = plane_sum(1)
            arrived(m.rs_in.at[1, 4], m.rs_recv.at[1, 4])
            m.mv[0] = total + m.rs_in[1, 4]

        mid_halo_go(0)

        @pl.when(root)
        def _():
            total = m.u_src[...]
            for i in range(4):
                arrived(m.u_in.at[i], m.u_recv.at[i])
                total = total + m.u_in[i]
            m.cv[1] = total

        coarse_send(1)

        @pl.when(plane)
        def _():
            arrived(m.a_buf, m.a_recv)
            for d in range(3):
                m.small[0, d] = stacked(m.a_buf[d])

        first = m.field.at[4]
        image(3, resid, first)
        halo_go(4, first, SLOTS * B)

        @pl.when(plane)
        def _():
            m.mv[1] = mid_image(0)

        mid_halo_go(1)

        @pl.when(root)
        def _():
            coarse_solve(1)

        for to in (1, 2, 3, 7):
            go(
                lambda to=to: copy(
                    m.fix.at[1], m.fix.at[1], m.fix_send.at[1, to], m.fix_recv.at[1], to
                ),
                root,
            )

        @pl.when(plane)
        def _():
            m.mid_src[...] = COEF_ZERO * m.mv[0] + COEF_ONE * m.mv[1] + COEF_TWO * mid_image(1)

        @pl.when(plane & jnp.logical_not(root))
        def _():
            arrived(m.fix.at[1], m.fix_recv.at[1])

        @pl.when(plane)
        def _():
            value = m.mid_src[...] + product(m.p_part[...], beside(m.fix[1]))
            m.mid_src[...] = value
            m.fbuf[1, lvl] = value + m.fix[1]

        gather_go(1)
        go(
            lambda: copy(m.fbuf.at[1, lvl], m.fbuf.at[1, lvl], m.f_send.at[0, 0], m.f_recv.at[1, lvl], 4),
            plane,
        )
        go(
            lambda: copy(
                m.mid_src, m.mid_out.at[lax.rem(lvl, 2)], m.mid_send, m.mid_out_recv.at[lax.rem(lvl, 2)],
                5 + lvl // 2,
            ),
            plane,
        )
        image(4, first, m.smooth)
        m.smooth[...] = m.sol[...] + blend(resid, first)

        @pl.when(plane)
        def _():
            for step in range(1, 4):
                source = lax.rem(lvl + step, 4)
                arrived(m.fbuf.at[1, source], m.f_recv.at[1, source])

        @pl.when(four)
        def _():
            for k in range(4):
                arrived(m.fbuf.at[1, k], m.f_recv.at[1, k])

        correct(1, out)
        drain()

    @pl.when(is_mid)
    def _():
        pair = lvl - 5
        load_links.wait()
        eye = (
            lax.broadcasted_iota(jnp.int32, (B, B), 0) == lax.broadcasted_iota(jnp.int32, (B, B), 1)
        ).astype(F32)
        for p in range(2):
            tile = m.links[2 * p, 0] + 0.5 * eye
            m.t_src[p] = tile
            m.link_parts[2 * p, 0] = stacked(tile)
            m.link_parts[2 * p, 1] = stacked(m.links[2 * p, 1])
        load_rhs.wait()
        meet()
        for p in range(2):
            k = 2 * pair + p
            go(lambda p=p, k=k: copy(m.t_src.at[p], m.t_buf.at[k], m.t_send.at[p], m.t_recv.at[k], k))
            go(lambda p=p, k=k: copy(m.t_src.at[p], m.t_buf.at[k], m.t_send.at[2 + p], m.t_recv.at[k], 4))
        for p in range(2):
            k = 2 * pair + p
            go(lambda p=p, k=k: copy(m.links.at[2 * p, 1], m.p_buf, m.p_send.at[p], m.p_recv, k))
        load_ops.wait()
        for p in range(2):
            for d in range(3):
                tile = gathered_tile(2 * p, d * SLOTS + 2 * p)
                m.a_src[p, d] = tile
                m.small[p, d] = stacked(tile)

        def level_image(turn, dst):
            for p in range(2):
                part = pl.ds(p * B, B)
                dst[part] = product(m.small[p, 1], beside(m.field[turn, part]))
            for side in range(2):
                @pl.when(has[side])
                def _():
                    halo_arrived(turn, side, 2 * B)
                    for p in range(2):
                        part = pl.ds(p * B, B)
                        dst[part] = dst[part] + product(
                            m.small[p, 2 * side], beside(m.halo[turn, side, part])
                        )

        for p in range(2):
            for source in (1, 0):
                arrived(m.mid_in.at[p, source], m.mid_recv.at[p, source])
            m.field[0, pl.ds(p * B, B)] = m.mid_in[p, 0] + m.mid_in[p, 1]
        total = product(m.link_parts[0, 0], beside(m.field[0, pl.ds(0, B)]))
        m.part_src[...] = total + product(m.link_parts[2, 0], beside(m.field[0, pl.ds(B, B)]))
        go(lambda: copy(m.part_src, m.coarse_in.at[pair], m.part_send, m.coarse_recv.at[pair], 7))
        halo_go(0, m.field.at[0], 2 * B)
        level_image(0, m.field.at[1])
        halo_go(1, m.field.at[1], 2 * B)
        level_image(1, m.smooth)
        part = pl.ds(0, 2 * B)
        m.smooth[part] = (
            COEF_ZERO * m.field[0, part] + COEF_ONE * m.field[1, part] + COEF_TWO * m.smooth[part]
        )
        arrived(m.fix.at[0], m.fix_recv.at[0])
        coarse = beside(m.fix[0])
        for p in range(2):
            k = 2 * pair + p
            value = m.smooth[pl.ds(p * B, B)] + product(m.link_parts[2 * p, 1], coarse)
            m.fbuf[0, k] = value + m.fix[0]
            for way, to in enumerate((k, 4)):
                go(
                    lambda k=k, p=p, way=way, to=to: copy(
                        m.fbuf.at[0, k], m.fbuf.at[0, k], m.f_send.at[p, way], m.f_recv.at[0, k], to
                    )
                )
        for p in range(2):
            k = 2 * pair + p
            go(lambda p=p, k=k: copy(m.a_src.at[p], m.a_buf, m.a_send.at[p], m.a_recv, k))
        out[pl.ds(B, B)] = jnp.zeros((B, B), F32)
        for p in range(2):
            arrived(m.mid_out.at[p], m.mid_out_recv.at[p])
            out[pl.ds(2 * p * B, B)] = m.mid_out[p]
        drain()

    @pl.when(is_coarse)
    def _():
        load_links.wait()
        load_rhs.wait()
        load_ops.wait()
        for d in range(3):
            m.ac[d] = gathered_tile(1, d * SLOTS + 1)
        clear_missing(m.chalo.at[0], has_far)
        meet()
        for side in range(2):
            go(
                lambda side=side: copy(
                    m.ac, m.ahalo.at[1 - side], m.ahalo_send.at[side], m.ahalo_recv.at[1 - side], lvl, near[side]
                ),
                has[side],
            )
        eye = (
            lax.broadcasted_iota(jnp.int32, (B, B), 0) == lax.broadcasted_iota(jnp.int32, (B, B), 1)
        ).astype(F32)
        centre = stacked(m.ac[1])
        m.st[0] = jnp.zeros((B, B), F32)
        m.st[1] = COEF_ONE * m.ac[0] + COEF_TWO * product(centre, beside(m.ac[0]))
        m.st[2] = COEF_ZERO * eye + COEF_ONE * m.ac[1] + COEF_TWO * product(centre, beside(m.ac[1]))
        m.st[3] = COEF_ONE * m.ac[2] + COEF_TWO * product(centre, beside(m.ac[2]))
        m.st[4] = jnp.zeros((B, B), F32)
        for side in range(2):
            @pl.when(has[side])
            def _():
                arrived(m.ahalo.at[side], m.ahalo_recv.at[side])
                edge = stacked(m.ac[2 * side])
                for d in range(3):
                    to = 2 * side + d
                    m.st[to] = m.st[to] + COEF_TWO * product(edge, beside(m.ahalo[side, d]))
        split_stencil()
        for pair in range(2):
            arrived(m.coarse_in.at[pair], m.coarse_recv.at[pair])
        m.cv[0] = m.coarse_in[0] + m.coarse_in[1]
        coarse_send(0)
        coarse_solve(0)
        for pair in range(2):
            go(
                lambda pair=pair: copy(
                    m.fix.at[0], m.fix.at[0], m.fix_send.at[0, pair], m.fix_recv.at[0], 5 + pair
                )
            )
        go(lambda: copy(m.st, m.st, m.st_send, m.st_recv, 0))
        out[pl.ds(0, B)] = jnp.zeros((B, B), F32)
        out[pl.ds(2 * B, B)] = jnp.zeros((B, B), F32)
        arrived(m.fix.at[1], m.fix_recv.at[1])
        out[pl.ds(B, B)] = m.fix[1]
        drain()


def scratch():
    dma = lambda *shape: pltpu.SemaphoreType.DMA(shape)
    block = lambda *lead: pltpu.VMEM(lead + (B, B), F32)
    slab = lambda *lead: pltpu.VMEM(lead + (SLOTS * B, B), F32)
    parts = lambda *lead: pltpu.VMEM(lead + (2 * B, B), BF16)
    return dict(
        rhs=slab(), ops=block(SLOTS * OPT), links=block(SLOTS, 2),
        wide=pltpu.VMEM((3, 2 * SLOTS * B, SLOTS * B), BF16), small=parts(2, 3), link_parts=parts(SLOTS, 2),
        field=slab(5), halo=slab(5, 2), sol=slab(), smooth=slab(),
        rs_src=block(2, 4), rs_in=block(2, 5), sum_src=block(), mid_in=block(2, 2),
        part_src=block(), coarse_in=block(2), fix=block(2), fbuf=block(2, 4),
        t_src=block(2), t_buf=block(4), t_part=parts(4), p_buf=block(), p_part=parts(),
        a_src=block(2, 3), a_buf=block(3), ac=block(3), ahalo=block(2, 3),
        st=block(5), st_own=parts(), st_far=pltpu.VMEM((2 * B, 4 * B), BF16),
        cv=block(2), chalo=block(2, 4), u_src=block(), u_in=block(4),
        mv=block(2), mhalo=block(2, 2), mid_src=block(), mid_out=block(2),
        in_sem=dma(3), halo_send=dma(5, 2), halo_recv=dma(5, 2),
        rs_send=dma(2, 4), rs_recv=dma(2, 5), sum_send=pltpu.SemaphoreType.DMA, mid_recv=dma(2, 2),
        four_send=dma(8), part_send=pltpu.SemaphoreType.DMA, coarse_recv=dma(2),
        fix_send=dma(2, 8), fix_recv=dma(2), f_send=dma(2, 2), gather_send=dma(2, 4), f_recv=dma(2, 4),
        t_send=dma(4), t_recv=dma(4), p_send=dma(2), p_recv=pltpu.SemaphoreType.DMA,
        a_send=dma(2), a_recv=pltpu.SemaphoreType.DMA, ahalo_send=dma(2), ahalo_recv=dma(2),
        st_send=pltpu.SemaphoreType.DMA, st_recv=pltpu.SemaphoreType.DMA,
        chalo_send=dma(2, 4), chalo_recv=dma(2, 4), u_send=pltpu.SemaphoreType.DMA, u_recv=dma(4),
        mhalo_send=dma(2, 2), mhalo_recv=dma(2, 2), mid_send=pltpu.SemaphoreType.DMA, mid_out_recv=dma(2),
    )


def solution(mesh):
    n_row = mesh.shape["row"]

    def per_device(rhs, op_tiles, op_cols, link_tiles, level_links):
        held = scratch()
        out = pl.pallas_call(
            functools.partial(kernel, n_row, tuple(held)),
            name="multigrid",
            out_shape=jax.ShapeDtypeStruct((SLOTS * B, B), F32),
            in_specs=[
                pl.BlockSpec(memory_space=pl.ANY),
                pl.BlockSpec(memory_space=pl.ANY),
                pl.BlockSpec(memory_space=pltpu.SMEM),
                pl.BlockSpec(memory_space=pl.ANY),
                pl.BlockSpec(memory_space=pltpu.SMEM),
            ],
            out_specs=pl.BlockSpec(memory_space=pltpu.VMEM),
            scratch_shapes=list(held.values()),
            compiler_params=pltpu.CompilerParams(
                collective_id=0, has_side_effects=True, vmem_limit_bytes=60 * 1024 * 1024
            ),
        )(
            rhs.reshape(SLOTS * B, B),
            op_tiles.reshape(SLOTS * OPT, B, B),
            op_cols.reshape(SLOTS * OPT),
            link_tiles.reshape(SLOTS, 2, B, B),
            level_links.reshape(SLOTS * 2),
        )
        return out.reshape(1, 1, SLOTS, B, B)

    placed = (
        P("lvl", "row", None, None, None),
        P("lvl", "row", None, None, None, None),
        P("lvl", "row", None, None),
        P("lvl", "row", None, None, None, None),
        P("lvl", "row", None, None),
    )
    return jax.shard_map(
        per_device,
        mesh=mesh,
        in_specs=placed,
        out_specs=P("lvl", "row", None, None, None),
        check_vma=False,
    )
```

```python
import functools
import types

import jax
import jax.numpy as jnp
from jax import lax
from jax.experimental import pallas as pl
from jax.experimental.pallas import tpu as pltpu
from jax.sharding import PartitionSpec as P

B = 128
SLOTS = 3
OPT = 7
COEF_ZERO = 0.9
COEF_ONE = -0.36
COEF_TWO = 0.05
MESH = pl.DeviceIdType.MESH
F32 = jnp.float32
BF16 = jnp.bfloat16


def halves(value):
    high = value.astype(BF16)
    return high, (value - high.astype(F32)).astype(BF16)


def stacked(value):
    return jnp.concatenate(halves(value), axis=0)


def beside(value):
    return jnp.concatenate(halves(value), axis=1)


def product(left, right):
    full = jnp.dot(left, right, preferred_element_type=F32)
    rows, columns = full.shape[0] // 2, full.shape[1] // 2
    cross = full[:rows, columns:] + full[rows:, :columns]
    return full[:rows, :columns] + (cross + full[rows:, columns:])


def kernel(n_row, names, rhs_hbm, ops_hbm, cols, links_hbm, targets, out, *refs):
    m = types.SimpleNamespace(**dict(zip(names, refs)))
    lvl = lax.axis_index("lvl")
    row = lax.axis_index("row")
    is_fine = lvl < 5
    is_mid = (lvl >= 5) & (lvl < 7)
    is_coarse = lvl == 7
    plane = lvl < 4
    four = lvl == 4
    root = lvl == 0
    has = (row > 0, row < n_row - 1)
    near = (row - 1, row + 1)
    far = (-2, -1, 1, 2)
    has_far = (row > 1, row > 0, row < n_row - 1, row < n_row - 2)

    load_rhs = pltpu.make_async_copy(rhs_hbm, m.rhs, m.in_sem.at[0])
    load_links = pltpu.make_async_copy(links_hbm, m.links, m.in_sem.at[1])
    load_ops = pltpu.make_async_copy(ops_hbm, m.ops, m.in_sem.at[2])
    for load in (load_rhs, load_links, load_ops):
        load.start()

    barrier = pltpu.get_barrier_semaphore()
    for step in range(1, 8):
        pl.semaphore_signal(
            barrier, inc=1, device_id={"lvl": lax.rem(lvl + step, 8), "row": row}, device_id_type=MESH
        )
    for step, there in zip(far, has_far):
        @pl.when(there)
        def _():
            pl.semaphore_signal(
                barrier, inc=1, device_id={"lvl": lvl, "row": row + step}, device_id_type=MESH
            )

    def meet():
        pl.semaphore_wait(barrier, 7 + sum(one.astype(jnp.int32) for one in has_far))

    pending = []

    def go(make, cond=None):
        pending.append((make, cond))
        if cond is None:
            make().start()
        else:
            pl.when(cond)(lambda: make().start())

    def drain():
        for make, cond in pending:
            if cond is None:
                make().wait_send()
            else:
                pl.when(cond)(lambda: make().wait_send())
        pending.clear()

    def copy(src, dst, send, recv, to_lvl, to_row=None):
        return pltpu.make_async_remote_copy(
            src_ref=src, dst_ref=dst, send_sem=send, recv_sem=recv,
            device_id={"lvl": to_lvl, "row": row if to_row is None else to_row},
            device_id_type=MESH,
        )

    def arrived(ref, sem):
        pltpu.make_async_copy(ref, ref, sem).wait()

    def halo_go(turn, src, rows):
        part = pl.ds(0, rows)
        for side in range(2):
            go(
                lambda side=side: copy(
                    src.at[part], m.halo.at[turn, 1 - side, part],
                    m.halo_send.at[turn, side], m.halo_recv.at[turn, 1 - side], lvl, near[side],
                ),
                has[side],
            )

    def halo_arrived(turn, side, rows):
        arrived(m.halo.at[turn, side, pl.ds(0, rows)], m.halo_recv.at[turn, side])

    def code_of(s, j):
        return cols[s * OPT + j]

    def gathered_tile(s, code):
        total = jnp.zeros((B, B), F32)
        for j in range(OPT):
            total = total + jnp.where(code_of(s, j) == code, F32(1), F32(0)) * m.ops[s * OPT + j]
        return total

    def clear_missing(ref, conditions):
        for i, there in enumerate(conditions):
            @pl.when(jnp.logical_not(there))
            def _():
                ref[i] = jnp.zeros((B, B), F32)

    def coarse_send(cycle):
        for i in range(4):
            go(
                lambda i=i: copy(
                    m.cv.at[cycle], m.chalo.at[cycle, 3 - i],
                    m.chalo_send.at[cycle, i], m.chalo_recv.at[cycle, 3 - i], lvl, row + far[i],
                ),
                has_far[i] & (is_coarse if cycle == 0 else root),
            )

    def coarse_solve(cycle):
        own = product(m.st_own[...], beside(m.cv[cycle]))
        for i in range(4):
            @pl.when(has_far[i])
            def _():
                arrived(m.chalo.at[cycle, i], m.chalo_recv.at[cycle, i])
        around = beside(m.chalo[cycle].reshape(4 * B, B))
        m.fix[cycle] = own + product(m.st_far[...], around)

    def split_stencil():
        m.st_own[...] = stacked(m.st[2])
        for i, d in enumerate((0, 1, 3, 4)):
            m.st_far[:, pl.ds(i * B, B)] = stacked(m.st[d])

    @pl.when(is_fine)
    def _():
        load_links.wait()
        for s in range(SLOTS):
            for kind in range(2):
                m.link_parts[s, kind] = stacked(m.links[s, kind])
        load_rhs.wait()

        def restrict(cycle, resid_of):
            terms = [
                product(m.link_parts[s, 0], beside(resid_of(s))) for s in range(SLOTS)
            ]
            for k in range(4):
                total = jnp.zeros((B, B), F32)
                for s in range(SLOTS):
                    hit = jnp.where(targets[s * 2] == k, F32(1), F32(0))
                    total = total + hit * terms[s]
                m.rs_src[cycle, k] = total
            return terms

        def send_terms(cycle):
            for step in range(1, 4):
                to = lax.rem(lvl + step, 4)
                go(
                    lambda step=step, to=to: copy(
                        m.rs_src.at[cycle, to], m.rs_in.at[cycle, lvl],
                        m.rs_send.at[cycle, step], m.rs_recv.at[cycle, lvl], to,
                    ),
                    plane,
                )

        def plane_sum(cycle):
            total = m.rs_src[cycle, lvl]
            for step in range(1, 4):
                source = lax.rem(lvl + step, 4)
                arrived(m.rs_in.at[cycle, source], m.rs_recv.at[cycle, source])
                total = total + m.rs_in[cycle, source]
            return total

        def gather_go(cycle):
            for step in range(1, 4):
                go(
                    lambda step=step: copy(
                        m.fbuf.at[cycle, lvl], m.fbuf.at[cycle, lvl],
                        m.gather_send.at[cycle, step], m.f_recv.at[cycle, lvl], lax.rem(lvl + step, 4),
                    ),
                    plane,
                )

        def image(turn, src, dst):
            dst[...] = product(m.wide[1], beside(src[...]))
            for side in range(2):
                @pl.when(has[side])
                def _():
                    halo_arrived(turn, side, SLOTS * B)
                    dst[...] = dst[...] + product(m.wide[2 * side], beside(m.halo[turn, side]))

        def raise_fix(cycle):
            coarse = beside(m.fix[cycle])
            for s in range(SLOTS):
                m.lift[s] = m.fix[cycle] + product(m.p_part[targets[s * 2 + 1]], coarse)

        def correct(cycle, dest):
            for s in range(SLOTS):
                chosen = m.lift[s] + m.fbuf[cycle, targets[s * 2 + 1]]
                rows = pl.ds(s * B, B)
                dest[rows] = m.smooth[rows] + product(m.link_parts[s, 1], beside(chosen))

        def blend(resid, first):
            return COEF_ZERO * resid[...] + COEF_ONE * first[...] + COEF_TWO * m.smooth[...]

        restrict(0, lambda s: m.rhs[pl.ds(s * B, B)])
        meet()
        send_terms(0)
        for k in range(4):
            go(
                lambda k=k: copy(
                    m.rs_src.at[0, k], m.mid_in.at[k % 2, 1],
                    m.four_send.at[k], m.mid_recv.at[k % 2, 1], 5 + k // 2,
                ),
                four,
            )
        halo_go(0, m.rhs, SLOTS * B)

        load_ops.wait()

        def dense(s, carry):
            for code in range(3 * SLOTS):
                high, low = halves(gathered_tile(s, code))
                columns = pl.ds((code % SLOTS) * B, B)
                m.wide[code // SLOTS, pl.ds(pl.multiple_of(s * B, B), B), columns] = high
                m.wide[code // SLOTS, pl.ds(pl.multiple_of((SLOTS + s) * B, B), B), columns] = low
            return carry

        lax.fori_loop(0, SLOTS, dense, 0)

        sum_copy = lambda: copy(
            m.sum_src, m.mid_in.at[lax.rem(lvl, 2), 0],
            m.sum_send, m.mid_recv.at[lax.rem(lvl, 2), 0], 5 + lvl // 2,
        )

        @pl.when(plane)
        def _():
            m.sum_src[...] = plane_sum(0)
            sum_copy().start()

        first = m.field.at[1]
        image(0, m.rhs, first)

        @pl.when(plane)
        def _():
            sum_copy().wait_send()

        halo_go(1, first, SLOTS * B)

        @pl.when(four)
        def _():
            arrived(m.t_buf.at[0], m.t_recv.at[0])
            arrived(m.p_buf.at[0], m.p_recv.at[0])
            arrived(m.a_buf, m.a_recv)

        go(lambda: copy(m.p_buf.at[0], m.p_buf.at[0], m.hop_send.at[0], m.p_recv.at[0], 0), four)
        go(lambda: copy(m.t_buf.at[0], m.t_buf.at[0], m.hop_send.at[1], m.t_recv.at[0], 0), four)
        go(lambda: copy(m.a_buf, m.a_buf, m.hop_send.at[2], m.a_recv, 0), four)
        image(1, first, m.smooth)
        m.smooth[...] = blend(m.rhs, first)

        for buf, send, recv in ((m.p_buf, m.p_send, m.p_recv), (m.t_buf, m.t_send, m.t_recv)):
            @pl.when(plane)
            def _():
                arrived(buf.at[lvl], recv.at[lvl])

            for step in range(1, 4):
                go(
                    lambda step=step, buf=buf, send=send, recv=recv: copy(
                        buf.at[lvl], buf.at[lvl], send.at[step], recv.at[lvl], lax.rem(lvl + step, 4)
                    ),
                    plane,
                )

        @pl.when(plane)
        def _():
            for step in range(1, 4):
                source = lax.rem(lvl + step, 4)
                arrived(m.p_buf.at[source], m.p_recv.at[source])
                arrived(m.t_buf.at[source], m.t_recv.at[source])

        @pl.when(four)
        def _():
            for k in range(1, 4):
                arrived(m.p_buf.at[k], m.p_recv.at[k])
                arrived(m.t_buf.at[k], m.t_recv.at[k])

        for k in range(4):
            m.p_part[k] = stacked(m.p_buf[k])
            m.t_part[k] = stacked(m.t_buf[k])

        @pl.when(root)
        def _():
            arrived(m.st, m.st_recv)
            split_stencil()
            clear_missing(m.chalo.at[1], has_far)

        @pl.when(plane)
        def _():
            clear_missing(m.mhalo.at[0], has)
            clear_missing(m.mhalo.at[1], has)
            arrived(m.fbuf.at[0, lvl], m.f_recv.at[0, lvl])

        gather_go(0)

        @pl.when(four)
        def _():
            arrived(m.fbuf.at[0, 0], m.f_recv.at[0, 0])

        go(lambda: copy(m.fbuf.at[0, 0], m.fbuf.at[0, 0], m.hop_send.at[3], m.f_recv.at[0, 0], 0), four)
        arrived(m.fix.at[0], m.fix_recv.at[0])
        go(lambda: copy(m.fix.at[0], m.fix.at[0], m.hop_send.at[4], m.fix_recv.at[0], 0), four)
        raise_fix(0)

        @pl.when(plane)
        def _():
            for step in range(1, 4):
                source = lax.rem(lvl + step, 4)
                arrived(m.fbuf.at[0, source], m.f_recv.at[0, source])

        @pl.when(four)
        def _():
            for k in range(1, 4):
                arrived(m.fbuf.at[0, k], m.f_recv.at[0, k])

        correct(0, m.sol)

        halo_go(2, m.sol, SLOTS * B)
        image(2, m.sol, m.smooth)
        resid = m.field.at[3]
        resid[...] = m.rhs[...] - m.smooth[...]
        terms = restrict(1, lambda s: m.field[3, pl.ds(s * B, B)])
        send_terms(1)
        for k in range(1, 4):
            go(
                lambda k=k: copy(m.rs_src.at[1, k], m.hop_in, m.four_send.at[4 + k], m.hop_recv, 4 + k),
                four,
            )
        total = jnp.zeros((B, B), F32)
        for s in range(SLOTS):
            total = total + product(m.t_part[targets[s * 2]], beside(terms[s]))
        m.u_src[...] = total
        slot = jnp.maximum(lvl - 1, 0)
        go(
            lambda: copy(m.u_src, m.u_in.at[slot], m.u_send, m.u_recv.at[slot], 0),
            jnp.logical_not(root),
        )
        go(
            lambda: copy(m.rs_src.at[1, 0], m.rs_in.at[1, 4], m.four_send.at[4], m.rs_recv.at[1, 4], 0),
            four,
        )
        halo_go(3, resid, SLOTS * B)

        def mid_halo_go(turn):
            for side in range(2):
                go(
                    lambda side=side: copy(
                        m.mv.at[turn], m.mhalo.at[turn, 1 - side],
                        m.mhalo_send.at[turn, side], m.mhalo_recv.at[turn, 1 - side], lvl, near[side],
                    ),
                    has[side] & plane,
                )

        def mid_image(turn):
            own = product(m.small[0, 1], beside(m.mv[turn]))
            for side in range(2):
                @pl.when(has[side])
                def _():
                    arrived(m.mhalo.at[turn, side], m.mhalo_recv.at[turn, side])
            for side in range(2):
                own = own + product(m.small[0, 2 * side], beside(m.mhalo[turn, side]))
            return own

        @pl.when(plane)
        def _():
            total = plane_sum(1)
            arrived(m.rs_in.at[1, 4], m.rs_recv.at[1, 4])
            m.mv[0] = total + m.rs_in[1, 4]

        mid_halo_go(0)

        @pl.when(root)
        def _():
            total = m.u_src[...]
            for i in range(4):
                arrived(m.u_in.at[i], m.u_recv.at[i])
                total = total + m.u_in[i]
            m.cv[1] = total

        coarse_send(1)

        @pl.when(plane)
        def _():
            arrived(m.a_buf, m.a_recv)
            for d in range(3):
                m.small[0, d] = stacked(m.a_buf[d])

        first = m.field.at[4]
        image(3, resid, first)
        halo_go(4, first, SLOTS * B)

        @pl.when(plane)
        def _():
            m.mv[1] = mid_image(0)

        mid_halo_go(1)

        @pl.when(root)
        def _():
            coarse_solve(1)

        for to in (4, 2, 1, 3, 7):
            go(
                lambda to=to: copy(
                    m.fix.at[1], m.fix.at[1], m.fix_send.at[1, to], m.fix_recv.at[1], to
                ),
                root,
            )

        @pl.when(plane)
        def _():
            m.fbuf[1, lvl] = COEF_ZERO * m.mv[0] + COEF_ONE * m.mv[1] + COEF_TWO * mid_image(1)

        gather_go(1)
        go(
            lambda: copy(m.fbuf.at[1, lvl], m.fbuf.at[1, lvl], m.f_send.at[0, 0], m.f_recv.at[1, lvl], 4),
            plane,
        )
        image(4, first, m.smooth)
        m.smooth[...] = m.sol[...] + blend(resid, first)

        @pl.when(jnp.logical_not(root))
        def _():
            arrived(m.fix.at[1], m.fix_recv.at[1])

        @pl.when(plane)
        def _():
            m.mid_src[...] = m.fbuf[1, lvl] + product(m.p_part[lvl], beside(m.fix[1]))

        go(
            lambda: copy(
                m.mid_src, m.mid_out.at[lax.rem(lvl, 2)], m.mid_send, m.mid_out_recv.at[lax.rem(lvl, 2)],
                5 + lvl // 2,
            ),
            plane,
        )
        raise_fix(1)

        @pl.when(plane)
        def _():
            for step in range(1, 4):
                source = lax.rem(lvl + step, 4)
                arrived(m.fbuf.at[1, source], m.f_recv.at[1, source])

        @pl.when(four)
        def _():
            for k in range(4):
                arrived(m.fbuf.at[1, k], m.f_recv.at[1, k])

        correct(1, out)
        drain()

    def hop_up():
        arrived(m.hop_in, m.hop_recv)
        go(lambda: copy(m.hop_in, m.rs_in.at[1, 4], m.hop_send.at[1], m.rs_recv.at[1, 4], lvl - 4))

    @pl.when(is_mid)
    def _():
        pair = lvl - 5
        load_links.wait()
        eye = (
            lax.broadcasted_iota(jnp.int32, (B, B), 0) == lax.broadcasted_iota(jnp.int32, (B, B), 1)
        ).astype(F32)
        for p in range(2):
            tile = m.links[2 * p, 0] + 0.5 * eye
            m.t_src[p] = tile
            m.link_parts[2 * p, 0] = stacked(tile)
        load_rhs.wait()
        meet()
        def ship(src, dst, recv, send, k):
            go(lambda: copy(src, dst, send.at[0], recv, 4))
            go(lambda: copy(src, dst, send.at[1], recv, k + 4 * (k // 3)), k > 0)

        for p in range(2):
            k = 2 * pair + p
            ship(m.links.at[2 * p, 1], m.p_buf.at[k], m.p_recv.at[k], m.p_send.at[pl.ds(2 * p, 2)], k)
            ship(m.t_src.at[p], m.t_buf.at[k], m.t_recv.at[k], m.t_send.at[pl.ds(2 * p, 2)], k)
        load_ops.wait()
        for p in range(2):
            for d in range(3):
                tile = gathered_tile(2 * p, d * SLOTS + 2 * p)
                m.a_src[p, d] = tile
                m.small[p, d] = stacked(tile)
        for p in range(2):
            k = 2 * pair + p
            to = k + 4 * (1 - (lax.rem(k, 3) + 1) // 2)
            go(lambda p=p, to=to: copy(m.a_src.at[p], m.a_buf, m.a_send.at[p], m.a_recv, to))

        def level_image(turn, dst):
            for p in range(2):
                part = pl.ds(p * B, B)
                dst[part] = product(m.small[p, 1], beside(m.field[turn, part]))
            for side in range(2):
                @pl.when(has[side])
                def _():
                    halo_arrived(turn, side, 2 * B)
                    for p in range(2):
                        part = pl.ds(p * B, B)
                        dst[part] = dst[part] + product(
                            m.small[p, 2 * side], beside(m.halo[turn, side, part])
                        )

        for p in range(2):
            for source in (1, 0):
                arrived(m.mid_in.at[p, source], m.mid_recv.at[p, source])
            m.field[0, pl.ds(p * B, B)] = m.mid_in[p, 0] + m.mid_in[p, 1]
        total = product(m.link_parts[0, 0], beside(m.field[0, pl.ds(0, B)]))
        m.part_src[...] = total + product(m.link_parts[2, 0], beside(m.field[0, pl.ds(B, B)]))
        go(lambda: copy(m.part_src, m.coarse_in.at[pair], m.part_send, m.coarse_recv.at[pair], 7))
        halo_go(0, m.field.at[0], 2 * B)
        level_image(0, m.field.at[1])
        halo_go(1, m.field.at[1], 2 * B)
        level_image(1, m.smooth)
        part = pl.ds(0, 2 * B)
        m.smooth[part] = (
            COEF_ZERO * m.field[0, part] + COEF_ONE * m.field[1, part] + COEF_TWO * m.smooth[part]
        )
        for p in range(2):
            k = 2 * pair + p
            m.fbuf[0, k] = m.smooth[pl.ds(p * B, B)]
            ship(m.fbuf.at[0, k], m.fbuf.at[0, k], m.f_recv.at[0, k], m.f_send.at[p], k)
        arrived(m.fix.at[0], m.fix_recv.at[0])
        go(lambda: copy(m.fix.at[0], m.fix.at[0], m.hop_send.at[0], m.fix_recv.at[0], lvl - 4))
        hop_up()
        out[pl.ds(B, B)] = jnp.zeros((B, B), F32)
        for p in range(2):
            arrived(m.mid_out.at[p], m.mid_out_recv.at[p])
            out[pl.ds(2 * p * B, B)] = m.mid_out[p]
        drain()

    @pl.when(is_coarse)
    def _():
        load_links.wait()
        load_rhs.wait()
        load_ops.wait()
        for d in range(3):
            m.ac[d] = gathered_tile(1, d * SLOTS + 1)
        clear_missing(m.chalo.at[0], has_far)
        meet()
        for side in range(2):
            go(
                lambda side=side: copy(
                    m.ac, m.ahalo.at[1 - side], m.ahalo_send.at[side], m.ahalo_recv.at[1 - side], lvl, near[side]
                ),
                has[side],
            )
        eye = (
            lax.broadcasted_iota(jnp.int32, (B, B), 0) == lax.broadcasted_iota(jnp.int32, (B, B), 1)
        ).astype(F32)
        centre = stacked(m.ac[1])
        m.st[0] = jnp.zeros((B, B), F32)
        m.st[1] = COEF_ONE * m.ac[0] + COEF_TWO * product(centre, beside(m.ac[0]))
        m.st[2] = COEF_ZERO * eye + COEF_ONE * m.ac[1] + COEF_TWO * product(centre, beside(m.ac[1]))
        m.st[3] = COEF_ONE * m.ac[2] + COEF_TWO * product(centre, beside(m.ac[2]))
        m.st[4] = jnp.zeros((B, B), F32)
        for side in range(2):
            @pl.when(has[side])
            def _():
                arrived(m.ahalo.at[side], m.ahalo_recv.at[side])
                edge = stacked(m.ac[2 * side])
                for d in range(3):
                    to = 2 * side + d
                    m.st[to] = m.st[to] + COEF_TWO * product(edge, beside(m.ahalo[side, d]))
        go(lambda: copy(m.st, m.st, m.st_send, m.st_recv, 0))
        split_stencil()
        arrived(m.p_buf.at[3], m.p_recv.at[3])
        go(lambda: copy(m.p_buf.at[3], m.p_buf.at[3], m.p_send.at[0], m.p_recv.at[3], 3))
        arrived(m.t_buf.at[3], m.t_recv.at[3])
        go(lambda: copy(m.t_buf.at[3], m.t_buf.at[3], m.t_send.at[0], m.t_recv.at[3], 3))
        arrived(m.a_buf, m.a_recv)
        go(lambda: copy(m.a_buf, m.a_buf, m.a_send.at[0], m.a_recv, 3))
        for pair in range(2):
            arrived(m.coarse_in.at[pair], m.coarse_recv.at[pair])
        m.cv[0] = m.coarse_in[0] + m.coarse_in[1]
        coarse_send(0)
        coarse_solve(0)
        for to in (5, 4, 6, 3):
            go(
                lambda to=to: copy(
                    m.fix.at[0], m.fix.at[0], m.fix_send.at[0, to], m.fix_recv.at[0], to
                )
            )
        arrived(m.fbuf.at[0, 3], m.f_recv.at[0, 3])
        go(lambda: copy(m.fbuf.at[0, 3], m.fbuf.at[0, 3], m.f_send.at[0, 0], m.f_recv.at[0, 3], 3))
        hop_up()
        out[pl.ds(0, B)] = jnp.zeros((B, B), F32)
        out[pl.ds(2 * B, B)] = jnp.zeros((B, B), F32)
        arrived(m.fix.at[1], m.fix_recv.at[1])
        out[pl.ds(B, B)] = m.fix[1]
        drain()


def scratch():
    dma = lambda *shape: pltpu.SemaphoreType.DMA(shape)
    block = lambda *lead: pltpu.VMEM(lead + (B, B), F32)
    slab = lambda *lead: pltpu.VMEM(lead + (SLOTS * B, B), F32)
    parts = lambda *lead: pltpu.VMEM(lead + (2 * B, B), BF16)
    return dict(
        rhs=slab(), ops=block(SLOTS * OPT), links=block(SLOTS, 2),
        wide=pltpu.VMEM((3, 2 * SLOTS * B, SLOTS * B), BF16), small=parts(2, 3), link_parts=parts(SLOTS, 2),
        field=slab(5), halo=slab(5, 2), sol=slab(), smooth=slab(),
        rs_src=block(2, 4), rs_in=block(2, 5), sum_src=block(), mid_in=block(2, 2),
        part_src=block(), coarse_in=block(2), fix=block(2), fbuf=block(2, 4),
        t_src=block(2), t_buf=block(4), t_part=parts(4), p_buf=block(4), p_part=parts(4), lift=block(SLOTS), hop_in=block(),
        a_src=block(2, 3), a_buf=block(3), ac=block(3), ahalo=block(2, 3),
        st=block(5), st_own=parts(), st_far=pltpu.VMEM((2 * B, 4 * B), BF16),
        cv=block(2), chalo=block(2, 4), u_src=block(), u_in=block(4),
        mv=block(2), mhalo=block(2, 2), mid_src=block(), mid_out=block(2),
        in_sem=dma(3), halo_send=dma(5, 2), halo_recv=dma(5, 2),
        rs_send=dma(2, 4), rs_recv=dma(2, 5), sum_send=pltpu.SemaphoreType.DMA, mid_recv=dma(2, 2),
        four_send=dma(8), part_send=pltpu.SemaphoreType.DMA, coarse_recv=dma(2),
        fix_send=dma(2, 8), fix_recv=dma(2), f_send=dma(2, 2), gather_send=dma(2, 4), f_recv=dma(2, 4),
        t_send=dma(4), t_recv=dma(4), p_send=dma(4), p_recv=dma(4), hop_send=dma(5), hop_recv=pltpu.SemaphoreType.DMA,
        a_send=dma(2), a_recv=pltpu.SemaphoreType.DMA, ahalo_send=dma(2), ahalo_recv=dma(2),
        st_send=pltpu.SemaphoreType.DMA, st_recv=pltpu.SemaphoreType.DMA,
        chalo_send=dma(2, 4), chalo_recv=dma(2, 4), u_send=pltpu.SemaphoreType.DMA, u_recv=dma(4),
        mhalo_send=dma(2, 2), mhalo_recv=dma(2, 2), mid_send=pltpu.SemaphoreType.DMA, mid_out_recv=dma(2),
    )


def solution(mesh):
    n_row = mesh.shape["row"]

    def per_device(rhs, op_tiles, op_cols, link_tiles, level_links):
        held = scratch()
        out = pl.pallas_call(
            functools.partial(kernel, n_row, tuple(held)),
            name="multigrid",
            out_shape=jax.ShapeDtypeStruct((SLOTS * B, B), F32),
            in_specs=[
                pl.BlockSpec(memory_space=pl.ANY),
                pl.BlockSpec(memory_space=pl.ANY),
                pl.BlockSpec(memory_space=pltpu.SMEM),
                pl.BlockSpec(memory_space=pl.ANY),
                pl.BlockSpec(memory_space=pltpu.SMEM),
            ],
            out_specs=pl.BlockSpec(memory_space=pltpu.VMEM),
            scratch_shapes=list(held.values()),
            compiler_params=pltpu.CompilerParams(
                collective_id=0, has_side_effects=True, vmem_limit_bytes=60 * 1024 * 1024
            ),
        )(
            rhs.reshape(SLOTS * B, B),
            op_tiles.reshape(SLOTS * OPT, B, B),
            op_cols.reshape(SLOTS * OPT),
            link_tiles.reshape(SLOTS, 2, B, B),
            level_links.reshape(SLOTS * 2),
        )
        return out.reshape(1, 1, SLOTS, B, B)

    placed = (
        P("lvl", "row", None, None, None),
        P("lvl", "row", None, None, None, None),
        P("lvl", "row", None, None),
        P("lvl", "row", None, None, None, None),
        P("lvl", "row", None, None),
    )
    return jax.shard_map(
        per_device,
        mesh=mesh,
        in_specs=placed,
        out_specs=P("lvl", "row", None, None, None),
        check_vma=False,
    )
```

```python
import functools
import types

import jax
import jax.numpy as jnp
from jax import lax
from jax.experimental import pallas as pl
from jax.experimental.pallas import tpu as pltpu
from jax.sharding import PartitionSpec as P

B = 128
SLOTS = 3
OPT = 7
COEF_ZERO = 0.9
COEF_ONE = -0.36
COEF_TWO = 0.05
MESH = pl.DeviceIdType.MESH
F32 = jnp.float32
BF16 = jnp.bfloat16


def halves(value):
    high = value.astype(BF16)
    return high, (value - high.astype(F32)).astype(BF16)


def stacked(value):
    return jnp.concatenate(halves(value), axis=0)


def beside(value):
    return jnp.concatenate(halves(value), axis=1)


def product(left, right):
    full = jnp.dot(left, right, preferred_element_type=F32)
    rows, columns = full.shape[0] // 2, full.shape[1] // 2
    cross = full[:rows, columns:] + full[rows:, :columns]
    return full[:rows, :columns] + (cross + full[rows:, columns:])


def kernel(n_row, names, rhs_hbm, ops_hbm, cols, links_hbm, targets, out, *refs):
    m = types.SimpleNamespace(**dict(zip(names, refs)))
    lvl = lax.axis_index("lvl")
    row = lax.axis_index("row")
    is_fine = lvl < 5
    is_mid = (lvl >= 5) & (lvl < 7)
    is_coarse = lvl == 7
    plane = lvl < 4
    four = lvl == 4
    root = lvl == 0
    has = (row > 0, row < n_row - 1)
    near = (row - 1, row + 1)
    far = (-2, -1, 1, 2)
    has_far = (row > 1, row > 0, row < n_row - 1, row < n_row - 2)

    load_rhs = pltpu.make_async_copy(rhs_hbm, m.rhs, m.in_sem.at[0])
    load_links = pltpu.make_async_copy(links_hbm, m.links, m.in_sem.at[1])
    load_ops = pltpu.make_async_copy(ops_hbm, m.ops, m.in_sem.at[2])
    for load in (load_rhs, load_links, load_ops):
        load.start()

    barrier = pltpu.get_barrier_semaphore()
    for step in range(1, 8):
        pl.semaphore_signal(
            barrier, inc=1, device_id={"lvl": lax.rem(lvl + step, 8), "row": row}, device_id_type=MESH
        )
    for step, there in zip(far, has_far):
        @pl.when(there)
        def _():
            pl.semaphore_signal(
                barrier, inc=1, device_id={"lvl": lvl, "row": row + step}, device_id_type=MESH
            )

    def meet():
        pl.semaphore_wait(barrier, 7 + sum(one.astype(jnp.int32) for one in has_far))

    pending = []

    def go(make, cond=None):
        pending.append((make, cond))
        if cond is None:
            make().start()
        else:
            pl.when(cond)(lambda: make().start())

    def drain():
        for make, cond in pending:
            if cond is None:
                make().wait_send()
            else:
                pl.when(cond)(lambda: make().wait_send())
        pending.clear()

    def copy(src, dst, send, recv, to_lvl, to_row=None):
        return pltpu.make_async_remote_copy(
            src_ref=src, dst_ref=dst, send_sem=send, recv_sem=recv,
            device_id={"lvl": to_lvl, "row": row if to_row is None else to_row},
            device_id_type=MESH,
        )

    def arrived(ref, sem):
        pltpu.make_async_copy(ref, ref, sem).wait()

    def halo_go(turn, src, rows):
        part = pl.ds(0, rows)
        for side in range(2):
            go(
                lambda side=side: copy(
                    src.at[part], m.halo.at[turn, 1 - side, part],
                    m.halo_send.at[turn, side], m.halo_recv.at[turn, 1 - side], lvl, near[side],
                ),
                has[side],
            )

    def halo_arrived(turn, side, rows):
        arrived(m.halo.at[turn, side, pl.ds(0, rows)], m.halo_recv.at[turn, side])

    def code_of(s, j):
        return cols[0, 0, s, j]

    def gathered_tile(s, code):
        total = jnp.zeros((B, B), F32)
        for j in range(OPT):
            total = total + jnp.where(code_of(s, j) == code, F32(1), F32(0)) * m.ops[s * OPT + j]
        return total

    def clear_missing(ref, conditions):
        for i, there in enumerate(conditions):
            @pl.when(jnp.logical_not(there))
            def _():
                ref[i] = jnp.zeros((B, B), F32)

    def side_go(turn, src, halo, send, recv, cond):
        for side in range(2):
            go(
                lambda side=side: copy(
                    src.at[turn], halo.at[turn, 1 - side],
                    send.at[turn, side], recv.at[turn, 1 - side], lvl, near[side],
                ),
                has[side] & cond,
            )

    def side_image(turn, parts, src, halo, recv):
        own = product(parts(1), beside(src[turn]))
        for side in range(2):
            @pl.when(has[side])
            def _():
                arrived(halo.at[turn, side], recv.at[turn, side])
        for side in range(2):
            own = own + product(parts(2 * side), beside(halo[turn, side]))
        return own

    @pl.when(is_fine)
    def _():
        load_links.wait()
        for s in range(SLOTS):
            for kind in range(2):
                m.link_parts[s, kind] = stacked(m.links[s, kind])
        load_rhs.wait()

        def restrict(cycle, resid_of):
            terms = [
                product(m.link_parts[s, 0], beside(resid_of(s))) for s in range(SLOTS)
            ]
            for k in range(4):
                total = jnp.zeros((B, B), F32)
                for s in range(SLOTS):
                    hit = jnp.where(targets[0, 0, s, 0] == k, F32(1), F32(0))
                    total = total + hit * terms[s]
                m.rs_src[cycle, k] = total
            return terms

        def send_terms(cycle):
            for step in range(1, 4):
                to = lax.rem(lvl + step, 4)
                go(
                    lambda step=step, to=to: copy(
                        m.rs_src.at[cycle, to], m.rs_in.at[cycle, lvl],
                        m.rs_send.at[cycle, step], m.rs_recv.at[cycle, lvl], to,
                    ),
                    plane,
                )

        def plane_sum(cycle):
            total = m.rs_src[cycle, lvl]
            for step in range(1, 4):
                source = lax.rem(lvl + step, 4)
                arrived(m.rs_in.at[cycle, source], m.rs_recv.at[cycle, source])
                total = total + m.rs_in[cycle, source]
            return total

        def gather_go(cycle):
            for step in range(1, 4):
                go(
                    lambda step=step: copy(
                        m.fbuf.at[cycle, lvl], m.fbuf.at[cycle, lvl],
                        m.gather_send.at[cycle, step], m.f_recv.at[cycle, lvl], lax.rem(lvl + step, 4),
                    ),
                    plane,
                )

        def image(turn, src, dst):
            dst[...] = product(m.wide[1], beside(src[...]))
            for side in range(2):
                @pl.when(has[side])
                def _():
                    halo_arrived(turn, side, SLOTS * B)
                    dst[...] = dst[...] + product(m.wide[2 * side], beside(m.halo[turn, side]))

        def raise_fix(cycle):
            coarse = beside(m.fix[cycle])
            for s in range(SLOTS):
                m.lift[s] = m.fix[cycle] + product(m.p_part[targets[0, 0, s, 1]], coarse)

        def correct(cycle, dest):
            for s in range(SLOTS):
                chosen = m.lift[s] + m.fbuf[cycle, targets[0, 0, s, 1]]
                rows = pl.ds(s * B, B)
                dest[rows] = m.smooth[rows] + product(m.link_parts[s, 1], beside(chosen))

        def blend(resid, first):
            return COEF_ZERO * resid[...] + COEF_ONE * first[...] + COEF_TWO * m.smooth[...]

        restrict(0, lambda s: m.rhs[pl.ds(s * B, B)])
        meet()
        send_terms(0)
        for k in range(4):
            go(
                lambda k=k: copy(
                    m.rs_src.at[0, k], m.mid_in.at[k % 2, 1],
                    m.four_send.at[k], m.mid_recv.at[k % 2, 1], 5 + k // 2,
                ),
                four,
            )
        halo_go(0, m.rhs, SLOTS * B)

        load_ops.wait()

        def dense(s, carry):
            for code in range(3 * SLOTS):
                high, low = halves(gathered_tile(s, code))
                columns = pl.ds((code % SLOTS) * B, B)
                m.wide[code // SLOTS, pl.ds(pl.multiple_of(s * B, B), B), columns] = high
                m.wide[code // SLOTS, pl.ds(pl.multiple_of((SLOTS + s) * B, B), B), columns] = low
            return carry

        lax.fori_loop(0, SLOTS, dense, 0)

        sum_copy = lambda: copy(
            m.sum_src, m.mid_in.at[lax.rem(lvl, 2), 0],
            m.sum_send, m.mid_recv.at[lax.rem(lvl, 2), 0], 5 + lvl // 2,
        )

        @pl.when(plane)
        def _():
            m.sum_src[...] = plane_sum(0)
            sum_copy().start()

        first = m.field.at[1]
        image(0, m.rhs, first)

        @pl.when(plane)
        def _():
            sum_copy().wait_send()

        @pl.when(four)
        def _():
            arrived(m.p_buf.at[0], m.p_recv.at[0])
            arrived(m.t_buf.at[0], m.t_recv.at[0])

        go(lambda: copy(m.p_buf.at[0], m.p_buf.at[0], m.hop_send.at[0], m.p_recv.at[0], 0), four)
        go(lambda: copy(m.t_buf.at[0], m.t_buf.at[0], m.hop_send.at[1], m.t_recv.at[0], 0), four)
        halo_go(1, first, SLOTS * B)
        image(1, first, m.smooth)
        m.smooth[...] = blend(m.rhs, first)

        def spread_tile(buf, send, recv):
            @pl.when(plane)
            def _():
                arrived(buf.at[lvl], recv.at[lvl])

            for step in range(1, 4):
                go(
                    lambda step=step: copy(
                        buf.at[lvl], buf.at[lvl], send.at[step], recv.at[lvl], lax.rem(lvl + step, 4)
                    ),
                    plane,
                )

        spread_tile(m.p_buf, m.p_send, m.p_recv)

        @pl.when(four)
        def _():
            arrived(m.a_buf, m.a_recv)

        go(lambda: copy(m.a_buf, m.a_buf, m.hop_send.at[2], m.a_recv, 0), four)

        @pl.when(root)
        def _():
            clear_missing(m.khalo.at[0], has)
            clear_missing(m.khalo.at[1], has)

        @pl.when(plane)
        def _():
            clear_missing(m.mhalo.at[0], has)
            clear_missing(m.mhalo.at[1], has)
            arrived(m.fbuf.at[0, lvl], m.f_recv.at[0, lvl])

        gather_go(0)
        spread_tile(m.t_buf, m.t_send, m.t_recv)

        @pl.when(plane)
        def _():
            for step in range(1, 4):
                source = lax.rem(lvl + step, 4)
                arrived(m.p_buf.at[source], m.p_recv.at[source])

        @pl.when(four)
        def _():
            for k in range(1, 4):
                arrived(m.p_buf.at[k], m.p_recv.at[k])

        for k in range(4):
            m.p_part[k] = stacked(m.p_buf[k])

        arrived(m.fix.at[0], m.fix_recv.at[0])
        go(lambda: copy(m.fix.at[0], m.fix.at[0], m.hop_send.at[4], m.fix_recv.at[0], 0), four)
        raise_fix(0)

        @pl.when(plane)
        def _():
            for step in range(1, 4):
                source = lax.rem(lvl + step, 4)
                arrived(m.fbuf.at[0, source], m.f_recv.at[0, source])

        @pl.when(four)
        def _():
            for k in range(4):
                arrived(m.fbuf.at[0, k], m.f_recv.at[0, k])

        correct(0, m.sol)

        halo_go(2, m.sol, SLOTS * B)

        @pl.when(plane)
        def _():
            for step in range(1, 4):
                source = lax.rem(lvl + step, 4)
                arrived(m.t_buf.at[source], m.t_recv.at[source])

        @pl.when(four)
        def _():
            for k in range(1, 4):
                arrived(m.t_buf.at[k], m.t_recv.at[k])

        for k in range(4):
            m.t_part[k] = stacked(m.t_buf[k])

        image(2, m.sol, m.smooth)
        resid = m.field.at[3]
        resid[...] = m.rhs[...] - m.smooth[...]
        terms = restrict(1, lambda s: m.field[3, pl.ds(s * B, B)])
        send_terms(1)
        for k in range(1, 4):
            go(
                lambda k=k: copy(m.rs_src.at[1, k], m.hop_in, m.four_send.at[4 + k], m.hop_recv, 4 + k),
                four,
            )
        total = jnp.zeros((B, B), F32)
        for s in range(SLOTS):
            total = total + product(m.t_part[targets[0, 0, s, 0]], beside(terms[s]))
        m.u_src[...] = total
        slot = jnp.maximum(lvl - 1, 0)
        go(
            lambda: copy(m.u_src, m.u_in.at[slot], m.u_send, m.u_recv.at[slot], 0),
            jnp.logical_not(root),
        )
        go(
            lambda: copy(m.rs_src.at[1, 0], m.rs_in.at[1, 4], m.four_send.at[4], m.rs_recv.at[1, 4], 0),
            four,
        )
        halo_go(3, resid, SLOTS * B)

        mid_sides = (m.mv, m.mhalo, m.mhalo_send, m.mhalo_recv)
        top_sides = (m.kv, m.khalo, m.khalo_send, m.khalo_recv)

        def mid_image(turn):
            return side_image(turn, lambda d: m.small[0, d], m.mv, m.mhalo, m.mhalo_recv)

        def top_image(turn):
            return side_image(turn, lambda d: m.small[1, d], m.kv, m.khalo, m.khalo_recv)

        @pl.when(plane)
        def _():
            total = plane_sum(1)
            arrived(m.rs_in.at[1, 4], m.rs_recv.at[1, 4])
            m.mv[0] = total + m.rs_in[1, 4]

        side_go(0, *mid_sides, plane)

        @pl.when(root)
        def _():
            total = m.u_src[...]
            for i in range(4):
                arrived(m.u_in.at[i], m.u_recv.at[i])
                total = total + m.u_in[i]
            m.kv[0] = total

        side_go(0, *top_sides, root)

        @pl.when(plane)
        def _():
            arrived(m.a_buf, m.a_recv)
            for d in range(3):
                m.small[0, d] = stacked(m.a_buf[d])

        @pl.when(root)
        def _():
            arrived(m.ac, m.ac_recv)
            for d in range(3):
                m.small[1, d] = stacked(m.ac[d])

        first = m.field.at[4]
        image(3, resid, first)

        @pl.when(plane)
        def _():
            m.mv[1] = mid_image(0)

        side_go(1, *mid_sides, plane)

        @pl.when(root)
        def _():
            m.kv[1] = top_image(0)

        side_go(1, *top_sides, root)
        halo_go(4, first, SLOTS * B)

        @pl.when(root)
        def _():
            m.fix[1] = COEF_ZERO * m.kv[0] + COEF_ONE * m.kv[1] + COEF_TWO * top_image(1)

        for to in (4, 2, 1, 3):
            go(
                lambda to=to: copy(
                    m.fix.at[1], m.fix.at[1], m.fix_send.at[1, to], m.fix_recv.at[1], to
                ),
                root,
            )

        @pl.when(plane)
        def _():
            m.fbuf[1, lvl] = COEF_ZERO * m.mv[0] + COEF_ONE * m.mv[1] + COEF_TWO * mid_image(1)

        gather_go(1)
        go(
            lambda: copy(m.fbuf.at[1, lvl], m.fbuf.at[1, lvl], m.f_send.at[0, 0], m.f_recv.at[1, lvl], 4),
            plane,
        )
        go(
            lambda: copy(
                m.fbuf.at[1, lvl], m.mid_out.at[lax.rem(lvl, 2)], m.mid_send, m.mid_out_recv.at[lax.rem(lvl, 2)],
                5 + lvl // 2,
            ),
            plane & jnp.logical_not(root),
        )
        image(4, first, m.smooth)
        m.smooth[...] = m.sol[...] + blend(resid, first)

        @pl.when(jnp.logical_not(root))
        def _():
            arrived(m.fix.at[1], m.fix_recv.at[1])

        go(
            lambda: copy(m.fix.at[1], m.fix.at[1], m.fix_send.at[1, 5], m.fix_recv.at[1], lvl + 4),
            plane & jnp.logical_not(root),
        )
        raise_fix(1)

        @pl.when(plane)
        def _():
            for step in range(1, 4):
                source = lax.rem(lvl + step, 4)
                arrived(m.fbuf.at[1, source], m.f_recv.at[1, source])

        @pl.when(four)
        def _():
            arrived(m.fbuf.at[1, 0], m.f_recv.at[1, 0])

        go(lambda: copy(m.fbuf.at[1, 0], m.mid_out.at[0], m.mid_send, m.mid_out_recv.at[0], 5), four)

        @pl.when(four)
        def _():
            for k in range(1, 4):
                arrived(m.fbuf.at[1, k], m.f_recv.at[1, k])

        correct(1, out)
        drain()

    def hop_up():
        arrived(m.hop_in, m.hop_recv)
        go(lambda: copy(m.hop_in, m.rs_in.at[1, 4], m.hop_send.at[1], m.rs_recv.at[1, 4], lvl - 4))

    @pl.when(is_mid)
    def _():
        pair = lvl - 5
        load_links.wait()
        eye = (
            lax.broadcasted_iota(jnp.int32, (B, B), 0) == lax.broadcasted_iota(jnp.int32, (B, B), 1)
        ).astype(F32)
        for p in range(2):
            tile = m.links[2 * p, 0] + 0.5 * eye
            m.t_src[p] = tile
            m.link_parts[2 * p, 0] = stacked(tile)
            m.link_parts[2 * p, 1] = stacked(m.links[2 * p, 1])
        load_rhs.wait()
        meet()
        def smooth_go(p, way, to):
            k = 2 * pair + p
            go(lambda: copy(m.fbuf.at[0, k], m.fbuf.at[0, k], m.f_send.at[p, way], m.f_recv.at[0, k], to))

        def ship(src, dst, recv, send, k):
            go(lambda: copy(src, dst, send.at[0], recv, 4))
            go(lambda: copy(src, dst, send.at[1], recv, k + 4 * (k // 3)), k > 0)

        for p in range(2):
            k = 2 * pair + p
            ship(m.links.at[2 * p, 1], m.p_buf.at[k], m.p_recv.at[k], m.p_send.at[pl.ds(2 * p, 2)], k)
            ship(m.t_src.at[p], m.t_buf.at[k], m.t_recv.at[k], m.t_send.at[pl.ds(2 * p, 2)], k)
        load_ops.wait()
        for p in range(2):
            for d in range(3):
                tile = gathered_tile(2 * p, d * SLOTS + 2 * p)
                m.a_src[p, d] = tile
                m.small[p, d] = stacked(tile)
        for p in range(2):
            k = 2 * pair + p
            to = k + 4 * (1 - (lax.rem(k, 3) + 1) // 2)
            go(lambda p=p, to=to: copy(m.a_src.at[p], m.a_buf, m.a_send.at[p], m.a_recv, to))

        def level_image(turn, dst):
            for p in range(2):
                part = pl.ds(p * B, B)
                dst[part] = product(m.small[p, 1], beside(m.field[turn, part]))
            for side in range(2):
                @pl.when(has[side])
                def _():
                    halo_arrived(turn, side, 2 * B)
                    for p in range(2):
                        part = pl.ds(p * B, B)
                        dst[part] = dst[part] + product(
                            m.small[p, 2 * side], beside(m.halo[turn, side, part])
                        )

        for p in range(2):
            for source in (1, 0):
                arrived(m.mid_in.at[p, source], m.mid_recv.at[p, source])
            m.field[0, pl.ds(p * B, B)] = m.mid_in[p, 0] + m.mid_in[p, 1]
        total = product(m.link_parts[0, 0], beside(m.field[0, pl.ds(0, B)]))
        m.part_src[...] = total + product(m.link_parts[2, 0], beside(m.field[0, pl.ds(B, B)]))
        go(lambda: copy(m.part_src, m.coarse_in.at[pair], m.part_send, m.coarse_recv.at[pair], 7))
        halo_go(0, m.field.at[0], 2 * B)
        level_image(0, m.field.at[1])
        halo_go(1, m.field.at[1], 2 * B)
        level_image(1, m.smooth)
        part = pl.ds(0, 2 * B)
        m.smooth[part] = (
            COEF_ZERO * m.field[0, part] + COEF_ONE * m.field[1, part] + COEF_TWO * m.smooth[part]
        )
        for p in range(2):
            k = 2 * pair + p
            m.fbuf[0, k] = m.smooth[pl.ds(p * B, B)]
            smooth_go(p, 0, k)
        arrived(m.fix.at[0], m.fix_recv.at[0])
        go(lambda: copy(m.fix.at[0], m.fix.at[0], m.hop_send.at[0], m.fix_recv.at[0], lvl - 4))
        for p in range(2):
            smooth_go(p, 1, 4)
        hop_up()
        out[pl.ds(B, B)] = jnp.zeros((B, B), F32)
        arrived(m.fix.at[1], m.fix_recv.at[1])
        for p in range(2):
            m.lift[p] = product(m.link_parts[2 * p, 1], beside(m.fix[1]))
        for p in range(2):
            arrived(m.mid_out.at[p], m.mid_out_recv.at[p])
            out[pl.ds(2 * p * B, B)] = m.mid_out[p] + m.lift[p]
        drain()

    @pl.when(is_coarse)
    def _():
        load_links.wait()
        load_rhs.wait()
        load_ops.wait()
        for d in range(3):
            m.ac[d] = gathered_tile(1, d * SLOTS + 1)
        clear_missing(m.chalo, has_far)
        meet()
        for side in range(2):
            go(
                lambda side=side: copy(
                    m.ac, m.ahalo.at[1 - side], m.ahalo_send.at[side], m.ahalo_recv.at[1 - side], lvl, near[side]
                ),
                has[side],
            )
        go(lambda: copy(m.ac, m.ac, m.st_send, m.ac_recv, 0))
        eye = (
            lax.broadcasted_iota(jnp.int32, (B, B), 0) == lax.broadcasted_iota(jnp.int32, (B, B), 1)
        ).astype(F32)
        centre = stacked(m.ac[1])
        m.st[0] = jnp.zeros((B, B), F32)
        m.st[1] = COEF_ONE * m.ac[0] + COEF_TWO * product(centre, beside(m.ac[0]))
        m.st[2] = COEF_ZERO * eye + COEF_ONE * m.ac[1] + COEF_TWO * product(centre, beside(m.ac[1]))
        m.st[3] = COEF_ONE * m.ac[2] + COEF_TWO * product(centre, beside(m.ac[2]))
        m.st[4] = jnp.zeros((B, B), F32)
        for side in range(2):
            @pl.when(has[side])
            def _():
                arrived(m.ahalo.at[side], m.ahalo_recv.at[side])
                edge = stacked(m.ac[2 * side])
                for d in range(3):
                    to = 2 * side + d
                    m.st[to] = m.st[to] + COEF_TWO * product(edge, beside(m.ahalo[side, d]))
        st_own = stacked(m.st[2])
        for i, d in enumerate((0, 1, 3, 4)):
            m.st_far[:, pl.ds(i * B, B)] = stacked(m.st[d])
        arrived(m.p_buf.at[3], m.p_recv.at[3])
        go(lambda: copy(m.p_buf.at[3], m.p_buf.at[3], m.p_send.at[0], m.p_recv.at[3], 3))
        for pair in range(2):
            arrived(m.coarse_in.at[pair], m.coarse_recv.at[pair])
        m.cv[...] = m.coarse_in[0] + m.coarse_in[1]
        for i in range(4):
            go(
                lambda i=i: copy(
                    m.cv, m.chalo.at[3 - i], m.chalo_send.at[i], m.chalo_recv.at[3 - i], lvl, row + far[i]
                ),
                has_far[i],
            )
        own = product(st_own, beside(m.cv[...]))
        for i in range(4):
            @pl.when(has_far[i])
            def _():
                arrived(m.chalo.at[i], m.chalo_recv.at[i])
        m.fix[0] = own + product(m.st_far[...], beside(m.chalo[...].reshape(4 * B, B)))
        for to in (5, 4, 6, 3):
            go(
                lambda to=to: copy(
                    m.fix.at[0], m.fix.at[0], m.fix_send.at[0, to], m.fix_recv.at[0], to
                )
            )
        arrived(m.t_buf.at[3], m.t_recv.at[3])
        go(lambda: copy(m.t_buf.at[3], m.t_buf.at[3], m.t_send.at[0], m.t_recv.at[3], 3))
        arrived(m.a_buf, m.a_recv)
        go(lambda: copy(m.a_buf, m.a_buf, m.a_send.at[0], m.a_recv, 3))
        hop_up()
        out[pl.ds(0, B)] = jnp.zeros((B, B), F32)
        out[pl.ds(2 * B, B)] = jnp.zeros((B, B), F32)
        arrived(m.fix.at[1], m.fix_recv.at[1])
        out[pl.ds(B, B)] = m.fix[1]
        drain()


def scratch():
    dma = lambda *shape: pltpu.SemaphoreType.DMA(shape)
    block = lambda *lead: pltpu.VMEM(lead + (B, B), F32)
    slab = lambda *lead: pltpu.VMEM(lead + (SLOTS * B, B), F32)
    parts = lambda *lead: pltpu.VMEM(lead + (2 * B, B), BF16)
    return dict(
        rhs=slab(), ops=block(SLOTS * OPT), links=block(SLOTS, 2),
        wide=pltpu.VMEM((3, 2 * SLOTS * B, SLOTS * B), BF16), small=parts(2, 3), link_parts=parts(SLOTS, 2),
        field=slab(5), halo=slab(5, 2), sol=slab(), smooth=slab(),
        rs_src=block(2, 4), rs_in=block(2, 5), sum_src=block(), mid_in=block(2, 2),
        part_src=block(), coarse_in=block(2), fix=block(2), fbuf=block(2, 4),
        t_src=block(2), t_buf=block(4), t_part=parts(4), p_buf=block(4), p_part=parts(4), lift=block(SLOTS), hop_in=block(),
        a_src=block(2, 3), a_buf=block(3), ac=block(3), ahalo=block(2, 3),
        st=block(5), st_far=pltpu.VMEM((2 * B, 4 * B), BF16),
        cv=block(), chalo=block(4), kv=block(2), khalo=block(2, 2), u_src=block(), u_in=block(4),
        mv=block(2), mhalo=block(2, 2), mid_out=block(2),
        in_sem=dma(3), halo_send=dma(5, 2), halo_recv=dma(5, 2),
        rs_send=dma(2, 4), rs_recv=dma(2, 5), sum_send=pltpu.SemaphoreType.DMA, mid_recv=dma(2, 2),
        four_send=dma(8), part_send=pltpu.SemaphoreType.DMA, coarse_recv=dma(2),
        fix_send=dma(2, 8), fix_recv=dma(2), f_send=dma(2, 2), gather_send=dma(2, 4), f_recv=dma(2, 4),
        t_send=dma(4), t_recv=dma(4), p_send=dma(4), p_recv=dma(4), hop_send=dma(5), hop_recv=pltpu.SemaphoreType.DMA,
        a_send=dma(2), a_recv=pltpu.SemaphoreType.DMA, ahalo_send=dma(2), ahalo_recv=dma(2),
        st_send=pltpu.SemaphoreType.DMA, ac_recv=pltpu.SemaphoreType.DMA,
        chalo_send=dma(4), chalo_recv=dma(4), khalo_send=dma(2, 2), khalo_recv=dma(2, 2), u_send=pltpu.SemaphoreType.DMA, u_recv=dma(4),
        mhalo_send=dma(2, 2), mhalo_recv=dma(2, 2), mid_send=pltpu.SemaphoreType.DMA, mid_out_recv=dma(2),
    )


def solution(mesh):
    n_row = mesh.shape["row"]

    def per_device(rhs, op_tiles, op_cols, link_tiles, level_links):
        held = scratch()
        out = pl.pallas_call(
            functools.partial(kernel, n_row, tuple(held)),
            name="multigrid",
            out_shape=jax.ShapeDtypeStruct((SLOTS * B, B), F32),
            in_specs=[
                pl.BlockSpec(memory_space=pl.ANY),
                pl.BlockSpec(memory_space=pl.ANY),
                pl.BlockSpec(memory_space=pltpu.SMEM),
                pl.BlockSpec(memory_space=pl.ANY),
                pl.BlockSpec(memory_space=pltpu.SMEM),
            ],
            out_specs=pl.BlockSpec(memory_space=pltpu.VMEM),
            scratch_shapes=list(held.values()),
            compiler_params=pltpu.CompilerParams(
                collective_id=0, has_side_effects=True, vmem_limit_bytes=60 * 1024 * 1024
            ),
        )(
            rhs.reshape(SLOTS * B, B),
            op_tiles.reshape(SLOTS * OPT, B, B),
            op_cols,
            link_tiles.reshape(SLOTS, 2, B, B),
            level_links,
        )
        return out.reshape(1, 1, SLOTS, B, B)

    placed = (
        P("lvl", "row", None, None, None),
        P("lvl", "row", None, None, None, None),
        P("lvl", "row", None, None),
        P("lvl", "row", None, None, None, None),
        P("lvl", "row", None, None),
    )
    return jax.shard_map(
        per_device,
        mesh=mesh,
        in_specs=placed,
        out_specs=P("lvl", "row", None, None, None),
        check_vma=False,
    )
```

```python
import functools
import types

import jax
import jax.numpy as jnp
from jax import lax
from jax.experimental import pallas as pl
from jax.experimental.pallas import tpu as pltpu
from jax.sharding import PartitionSpec as P

B = 128
SLOTS = 3
OPT = 7
COEF_ZERO = 0.9
COEF_ONE = -0.36
COEF_TWO = 0.05
MESH = pl.DeviceIdType.MESH
F32 = jnp.float32
BF16 = jnp.bfloat16


def halves(value):
    high = value.astype(BF16)
    return high, (value - high.astype(F32)).astype(BF16)


def stacked(value):
    return jnp.concatenate(halves(value), axis=0)


def beside(value):
    return jnp.concatenate(halves(value), axis=1)


def product(left, right):
    full = jnp.dot(left, right, preferred_element_type=F32)
    rows, columns = full.shape[0] // 2, full.shape[1] // 2
    cross = full[:rows, columns:] + full[rows:, :columns]
    return full[:rows, :columns] + (cross + full[rows:, columns:])


def kernel(n_row, names, rhs_hbm, ops_hbm, cols, links_hbm, targets, out, *refs):
    m = types.SimpleNamespace(**dict(zip(names, refs)))
    lvl = lax.axis_index("lvl")
    row = lax.axis_index("row")
    is_fine = lvl < 5
    is_mid = (lvl >= 5) & (lvl < 7)
    is_coarse = lvl == 7
    plane = lvl < 4
    four = lvl == 4
    root = lvl == 0
    has = (row > 0, row < n_row - 1)
    near = (row - 1, row + 1)
    far = (-2, -1, 1, 2)
    has_far = (row > 1, row > 0, row < n_row - 1, row < n_row - 2)

    load_rhs = pltpu.make_async_copy(rhs_hbm, m.rhs, m.in_sem.at[0])
    load_links = pltpu.make_async_copy(links_hbm, m.links, m.in_sem.at[1])
    load_ops = pltpu.make_async_copy(ops_hbm, m.ops, m.in_sem.at[2])
    for load in (load_rhs, load_links, load_ops):
        load.start()

    barrier = pltpu.get_barrier_semaphore()
    for step in range(1, 8):
        pl.semaphore_signal(
            barrier, inc=1, device_id={"lvl": lax.rem(lvl + step, 8), "row": row}, device_id_type=MESH
        )
    for step, there in zip(far, has_far):
        @pl.when(there)
        def _():
            pl.semaphore_signal(
                barrier, inc=1, device_id={"lvl": lvl, "row": row + step}, device_id_type=MESH
            )

    def meet():
        pl.semaphore_wait(barrier, 7 + sum(one.astype(jnp.int32) for one in has_far))

    pending = []

    def go(make, cond=None):
        pending.append((make, cond))
        if cond is None:
            make().start()
        else:
            pl.when(cond)(lambda: make().start())

    def drain():
        for make, cond in pending:
            if cond is None:
                make().wait_send()
            else:
                pl.when(cond)(lambda: make().wait_send())
        pending.clear()

    def copy(src, dst, send, recv, to_lvl, to_row=None):
        return pltpu.make_async_remote_copy(
            src_ref=src, dst_ref=dst, send_sem=send, recv_sem=recv,
            device_id={"lvl": to_lvl, "row": row if to_row is None else to_row},
            device_id_type=MESH,
        )

    def arrived(ref, sem):
        pltpu.make_async_copy(ref, ref, sem).wait()

    def halo_go(turn, src, rows):
        part = pl.ds(0, rows)
        for side in range(2):
            go(
                lambda side=side: copy(
                    src.at[part], m.halo.at[turn, 1 - side, part],
                    m.halo_send.at[turn, side], m.halo_recv.at[turn, 1 - side], lvl, near[side],
                ),
                has[side],
            )

    def halo_arrived(turn, side, rows):
        arrived(m.halo.at[turn, side, pl.ds(0, rows)], m.halo_recv.at[turn, side])

    def code_of(s, j):
        return cols[0, s, 0, j]

    def gathered_tile(s, code):
        total = jnp.zeros((B, B), F32)
        for j in range(OPT):
            total = total + jnp.where(code_of(s, j) == code, F32(1), F32(0)) * m.ops[s * OPT + j]
        return total

    def clear_missing(ref, conditions):
        for i, there in enumerate(conditions):
            @pl.when(jnp.logical_not(there))
            def _():
                ref[i] = jnp.zeros((B, B), F32)

    def side_go(turn, src, halo, send, recv, cond):
        for side in range(2):
            go(
                lambda side=side: copy(
                    src.at[turn], halo.at[turn, 1 - side],
                    send.at[turn, side], recv.at[turn, 1 - side], lvl, near[side],
                ),
                has[side] & cond,
            )

    def side_image(turn, parts, src, halo, recv):
        own = product(parts(1), beside(src[turn]))
        for side in range(2):
            @pl.when(has[side])
            def _():
                arrived(halo.at[turn, side], recv.at[turn, side])
        for side in range(2):
            own = own + product(parts(2 * side), beside(halo[turn, side]))
        return own

    @pl.when(is_fine)
    def _():
        load_links.wait()
        for s in range(SLOTS):
            for kind in range(2):
                m.link_parts[s, kind] = stacked(m.links[s, kind])
        load_rhs.wait()

        def restrict(cycle, resid_of):
            terms = [
                product(m.link_parts[s, 0], beside(resid_of(s))) for s in range(SLOTS)
            ]
            for k in range(4):
                total = jnp.zeros((B, B), F32)
                for s in range(SLOTS):
                    hit = jnp.where(targets[0, 0, 0, s] == k, F32(1), F32(0))
                    total = total + hit * terms[s]
                m.rs_src[cycle, k] = total
            return terms

        def send_terms(cycle):
            for step in range(1, 4):
                to = lax.rem(lvl + step, 4)
                go(
                    lambda step=step, to=to: copy(
                        m.rs_src.at[cycle, to], m.rs_in.at[cycle, lvl],
                        m.rs_send.at[cycle, step], m.rs_recv.at[cycle, lvl], to,
                    ),
                    plane,
                )

        def plane_sum(cycle):
            total = m.rs_src[cycle, lvl]
            for step in range(1, 4):
                source = lax.rem(lvl + step, 4)
                arrived(m.rs_in.at[cycle, source], m.rs_recv.at[cycle, source])
                total = total + m.rs_in[cycle, source]
            return total

        def gather_go(cycle):
            for step in range(1, 4):
                go(
                    lambda step=step: copy(
                        m.fbuf.at[cycle, lvl], m.fbuf.at[cycle, lvl],
                        m.gather_send.at[cycle, step], m.f_recv.at[cycle, lvl], lax.rem(lvl + step, 4),
                    ),
                    plane,
                )

        def image(turn, src, dst):
            dst[...] = product(m.wide[1], beside(src[...]))
            for side in range(2):
                @pl.when(has[side])
                def _():
                    halo_arrived(turn, side, SLOTS * B)
                    dst[...] = dst[...] + product(m.wide[2 * side], beside(m.halo[turn, side]))

        def raise_fix(cycle):
            coarse = beside(m.fix[cycle])
            for s in range(SLOTS):
                m.lift[s] = m.fix[cycle] + product(m.p_part[targets[0, 0, 1, s]], coarse)

        def correct(cycle, dest):
            for s in range(SLOTS):
                chosen = m.lift[s] + m.fbuf[cycle, targets[0, 0, 1, s]]
                rows = pl.ds(s * B, B)
                dest[rows] = m.smooth[rows] + product(m.link_parts[s, 1], beside(chosen))

        def blend(resid, first):
            return COEF_ZERO * resid[...] + COEF_ONE * first[...] + COEF_TWO * m.smooth[...]

        restrict(0, lambda s: m.rhs[pl.ds(s * B, B)])
        meet()
        send_terms(0)
        for k in range(4):
            go(
                lambda k=k: copy(
                    m.rs_src.at[0, k], m.mid_in.at[k % 2, 1],
                    m.four_send.at[k], m.mid_recv.at[k % 2, 1], 5 + k // 2,
                ),
                four,
            )
        halo_go(0, m.rhs, SLOTS * B)

        load_ops.wait()

        def dense(s, carry):
            for code in range(3 * SLOTS):
                high, low = halves(gathered_tile(s, code))
                columns = pl.ds((code % SLOTS) * B, B)
                m.wide[code // SLOTS, pl.ds(pl.multiple_of(s * B, B), B), columns] = high
                m.wide[code // SLOTS, pl.ds(pl.multiple_of((SLOTS + s) * B, B), B), columns] = low
            return carry

        lax.fori_loop(0, SLOTS, dense, 0)

        sum_copy = lambda: copy(
            m.sum_src, m.mid_in.at[lax.rem(lvl, 2), 0],
            m.sum_send, m.mid_recv.at[lax.rem(lvl, 2), 0], 5 + lvl // 2,
        )

        @pl.when(plane)
        def _():
            m.sum_src[...] = plane_sum(0)
            sum_copy().start()

        first = m.field.at[1]
        image(0, m.rhs, first)

        @pl.when(plane)
        def _():
            sum_copy().wait_send()

        @pl.when(four)
        def _():
            arrived(m.p_buf.at[0], m.p_recv.at[0])

        go(lambda: copy(m.p_buf.at[0], m.p_buf.at[0], m.hop_send.at[0], m.p_recv.at[0], 0), four)
        halo_go(1, first, SLOTS * B)
        image(1, first, m.smooth)
        m.smooth[...] = blend(m.rhs, first)

        def spread_tile(buf, send, recv):
            @pl.when(plane)
            def _():
                arrived(buf.at[lvl], recv.at[lvl])

            for step in range(1, 4):
                go(
                    lambda step=step: copy(
                        buf.at[lvl], buf.at[lvl], send.at[step], recv.at[lvl], lax.rem(lvl + step, 4)
                    ),
                    plane,
                )

        spread_tile(m.p_buf, m.p_send, m.p_recv)

        @pl.when(four)
        def _():
            arrived(m.a_buf, m.a_recv)

        go(lambda: copy(m.a_buf, m.a_buf, m.hop_send.at[2], m.a_recv, 0), four)

        @pl.when(root)
        def _():
            clear_missing(m.khalo.at[0], has)
            clear_missing(m.khalo.at[1], has)

        @pl.when(plane)
        def _():
            clear_missing(m.mhalo.at[0], has)
            clear_missing(m.mhalo.at[1], has)
            arrived(m.fbuf.at[0, lvl], m.f_recv.at[0, lvl])

        gather_go(0)

        @pl.when(plane)
        def _():
            for step in range(1, 4):
                source = lax.rem(lvl + step, 4)
                arrived(m.p_buf.at[source], m.p_recv.at[source])

        @pl.when(four)
        def _():
            for k in range(1, 4):
                arrived(m.p_buf.at[k], m.p_recv.at[k])

        for k in range(4):
            m.p_part[k] = stacked(m.p_buf[k])

        arrived(m.fix.at[0], m.fix_recv.at[0])
        go(lambda: copy(m.fix.at[0], m.fix.at[0], m.hop_send.at[4], m.fix_recv.at[0], 0), four)
        raise_fix(0)
        spread_tile(m.t_buf, m.t_send, m.t_recv)

        @pl.when(plane)
        def _():
            for step in range(1, 4):
                source = lax.rem(lvl + step, 4)
                arrived(m.fbuf.at[0, source], m.f_recv.at[0, source])

        @pl.when(four)
        def _():
            for k in range(4):
                arrived(m.fbuf.at[0, k], m.f_recv.at[0, k])

        correct(0, m.sol)

        halo_go(2, m.sol, SLOTS * B)

        image(2, m.sol, m.smooth)
        resid = m.field.at[3]
        resid[...] = m.rhs[...] - m.smooth[...]
        terms = restrict(1, lambda s: m.field[3, pl.ds(s * B, B)])
        send_terms(1)
        for k in range(1, 4):
            go(
                lambda k=k: copy(m.rs_src.at[1, k], m.hop_in, m.four_send.at[4 + k], m.hop_recv, 4 + k),
                four,
            )
        @pl.when(plane)
        def _():
            for step in range(1, 4):
                source = lax.rem(lvl + step, 4)
                arrived(m.t_buf.at[source], m.t_recv.at[source])

        @pl.when(four)
        def _():
            for k in range(4):
                arrived(m.t_buf.at[k], m.t_recv.at[k])

        for k in range(4):
            m.t_part[k] = stacked(m.t_buf[k])

        total = jnp.zeros((B, B), F32)
        for s in range(SLOTS):
            total = total + product(m.t_part[targets[0, 0, 0, s]], beside(terms[s]))
        m.u_src[...] = total
        slot = jnp.maximum(lvl - 1, 0)
        go(
            lambda: copy(m.u_src, m.u_in.at[slot], m.u_send, m.u_recv.at[slot], 0),
            jnp.logical_not(root),
        )
        go(
            lambda: copy(m.rs_src.at[1, 0], m.rs_in.at[1, 4], m.four_send.at[4], m.rs_recv.at[1, 4], 0),
            four,
        )
        halo_go(3, resid, SLOTS * B)

        mid_sides = (m.mv, m.mhalo, m.mhalo_send, m.mhalo_recv)
        top_sides = (m.kv, m.khalo, m.khalo_send, m.khalo_recv)

        def mid_image(turn):
            return side_image(turn, lambda d: m.small[0, d], m.mv, m.mhalo, m.mhalo_recv)

        def top_image(turn):
            return side_image(turn, lambda d: m.small[1, d], m.kv, m.khalo, m.khalo_recv)

        @pl.when(plane)
        def _():
            total = plane_sum(1)
            arrived(m.rs_in.at[1, 4], m.rs_recv.at[1, 4])
            m.mv[0] = total + m.rs_in[1, 4]

        side_go(0, *mid_sides, plane)

        @pl.when(root)
        def _():
            total = m.u_src[...]
            for i in range(4):
                arrived(m.u_in.at[i], m.u_recv.at[i])
                total = total + m.u_in[i]
            m.kv[0] = total

        side_go(0, *top_sides, root)

        @pl.when(plane)
        def _():
            arrived(m.a_buf, m.a_recv)
            for d in range(3):
                m.small[0, d] = stacked(m.a_buf[d])

        @pl.when(root)
        def _():
            arrived(m.ac, m.ac_recv)
            for d in range(3):
                m.small[1, d] = stacked(m.ac[d])

        first = m.field.at[4]
        image(3, resid, first)

        @pl.when(plane)
        def _():
            m.mv[1] = mid_image(0)

        side_go(1, *mid_sides, plane)

        @pl.when(root)
        def _():
            m.kv[1] = top_image(0)

        side_go(1, *top_sides, root)
        halo_go(4, first, SLOTS * B)

        @pl.when(plane)
        def _():
            m.fbuf[1, lvl] = COEF_ZERO * m.mv[0] + COEF_ONE * m.mv[1] + COEF_TWO * mid_image(1)

        gather_go(1)
        go(
            lambda: copy(m.fbuf.at[1, lvl], m.fbuf.at[1, lvl], m.f_send.at[0, 0], m.f_recv.at[1, lvl], 4),
            plane,
        )
        go(
            lambda: copy(
                m.fbuf.at[1, lvl], m.mid_out.at[lax.rem(lvl, 2)], m.mid_send, m.mid_out_recv.at[lax.rem(lvl, 2)],
                5 + lvl // 2,
            ),
            plane & jnp.logical_not(root),
        )
        @pl.when(root)
        def _():
            m.fix[1] = COEF_ZERO * m.kv[0] + COEF_ONE * m.kv[1] + COEF_TWO * top_image(1)

        for to in (4, 2, 1, 3):
            go(
                lambda to=to: copy(
                    m.fix.at[1], m.fix.at[1], m.fix_send.at[1, to], m.fix_recv.at[1], to
                ),
                root,
            )

        image(4, first, m.smooth)
        m.smooth[...] = m.sol[...] + blend(resid, first)

        @pl.when(four)
        def _():
            arrived(m.fbuf.at[1, 0], m.f_recv.at[1, 0])

        go(lambda: copy(m.fbuf.at[1, 0], m.mid_out.at[0], m.mid_send, m.mid_out_recv.at[0], 5), four)

        @pl.when(jnp.logical_not(root))
        def _():
            arrived(m.fix.at[1], m.fix_recv.at[1])

        go(
            lambda: copy(m.fix.at[1], m.fix.at[1], m.fix_send.at[1, 5], m.fix_recv.at[1], lvl + 4),
            plane & jnp.logical_not(root),
        )
        raise_fix(1)

        @pl.when(plane)
        def _():
            for step in range(1, 4):
                source = lax.rem(lvl + step, 4)
                arrived(m.fbuf.at[1, source], m.f_recv.at[1, source])

        @pl.when(four)
        def _():
            for k in range(1, 4):
                arrived(m.fbuf.at[1, k], m.f_recv.at[1, k])

        correct(1, out)
        drain()

    def hop_up():
        arrived(m.hop_in, m.hop_recv)
        go(lambda: copy(m.hop_in, m.rs_in.at[1, 4], m.hop_send.at[1], m.rs_recv.at[1, 4], lvl - 4))

    @pl.when(is_mid)
    def _():
        pair = lvl - 5
        load_links.wait()
        eye = (
            lax.broadcasted_iota(jnp.int32, (B, B), 0) == lax.broadcasted_iota(jnp.int32, (B, B), 1)
        ).astype(F32)
        for p in range(2):
            tile = m.links[2 * p, 0] + 0.5 * eye
            m.t_src[p] = tile
            m.link_parts[2 * p, 0] = stacked(tile)
            m.link_parts[2 * p, 1] = stacked(m.links[2 * p, 1])
        load_rhs.wait()
        meet()
        def smooth_go(p, way, to):
            k = 2 * pair + p
            go(lambda: copy(m.fbuf.at[0, k], m.fbuf.at[0, k], m.f_send.at[p, way], m.f_recv.at[0, k], to))

        def ship(src, dst, recv, send, k):
            go(lambda: copy(src, dst, send.at[0], recv, 4))
            go(lambda: copy(src, dst, send.at[1], recv, k), k > 0)

        for p in range(2):
            k = 2 * pair + p
            ship(m.links.at[2 * p, 1], m.p_buf.at[k], m.p_recv.at[k], m.p_send.at[pl.ds(2 * p, 2)], k)
        load_ops.wait()
        for p in range(2):
            for d in range(3):
                tile = gathered_tile(2 * p, d * SLOTS + 2 * p)
                m.a_src[p, d] = tile
                m.small[p, d] = stacked(tile)
        for p in range(2):
            k = 2 * pair + p
            to = k + 4 * (1 - (lax.rem(k, 3) + 1) // 2)
            go(lambda p=p, to=to: copy(m.a_src.at[p], m.a_buf, m.a_send.at[p], m.a_recv, to))
        for p in range(2):
            k = 2 * pair + p
            go(
                lambda p=p, k=k: copy(
                    m.t_src.at[p], m.t_buf.at[k], m.t_send.at[p], m.t_recv.at[k], k
                )
            )

        def level_image(turn, dst):
            for p in range(2):
                part = pl.ds(p * B, B)
                dst[part] = product(m.small[p, 1], beside(m.field[turn, part]))
            for side in range(2):
                @pl.when(has[side])
                def _():
                    halo_arrived(turn, side, 2 * B)
                    for p in range(2):
                        part = pl.ds(p * B, B)
                        dst[part] = dst[part] + product(
                            m.small[p, 2 * side], beside(m.halo[turn, side, part])
                        )

        for p in range(2):
            for source in (1, 0):
                arrived(m.mid_in.at[p, source], m.mid_recv.at[p, source])
            m.field[0, pl.ds(p * B, B)] = m.mid_in[p, 0] + m.mid_in[p, 1]
        total = product(m.link_parts[0, 0], beside(m.field[0, pl.ds(0, B)]))
        m.part_src[...] = total + product(m.link_parts[2, 0], beside(m.field[0, pl.ds(B, B)]))
        go(lambda: copy(m.part_src, m.coarse_in.at[pair], m.part_send, m.coarse_recv.at[pair], 7))
        halo_go(0, m.field.at[0], 2 * B)
        level_image(0, m.field.at[1])
        halo_go(1, m.field.at[1], 2 * B)
        level_image(1, m.smooth)
        part = pl.ds(0, 2 * B)
        m.smooth[part] = (
            COEF_ZERO * m.field[0, part] + COEF_ONE * m.field[1, part] + COEF_TWO * m.smooth[part]
        )
        for p in range(2):
            k = 2 * pair + p
            m.fbuf[0, k] = m.smooth[pl.ds(p * B, B)]
            smooth_go(p, 0, k)
        for p in range(2):
            smooth_go(p, 1, 4)
        arrived(m.fix.at[0], m.fix_recv.at[0])
        go(lambda: copy(m.fix.at[0], m.fix.at[0], m.hop_send.at[0], m.fix_recv.at[0], lvl - 4))
        for p in range(2):
            k = 2 * pair + p
            go(lambda p=p, k=k: copy(m.t_src.at[p], m.t_buf.at[k], m.t_send.at[2 + p], m.t_recv.at[k], 4))
        hop_up()
        out[pl.ds(B, B)] = jnp.zeros((B, B), F32)
        arrived(m.fix.at[1], m.fix_recv.at[1])
        for p in range(2):
            m.lift[p] = product(m.link_parts[2 * p, 1], beside(m.fix[1]))
        for p in range(2):
            arrived(m.mid_out.at[p], m.mid_out_recv.at[p])
            out[pl.ds(2 * p * B, B)] = m.mid_out[p] + m.lift[p]
        drain()

    @pl.when(is_coarse)
    def _():
        load_links.wait()
        load_rhs.wait()
        load_ops.wait()
        for d in range(3):
            m.ac[d] = gathered_tile(1, d * SLOTS + 1)
        clear_missing(m.chalo, has_far)
        meet()
        for side in range(2):
            go(
                lambda side=side: copy(
                    m.ac, m.ahalo.at[1 - side], m.ahalo_send.at[side], m.ahalo_recv.at[1 - side], lvl, near[side]
                ),
                has[side],
            )
        go(lambda: copy(m.ac, m.ac, m.st_send, m.ac_recv, 0))
        eye = (
            lax.broadcasted_iota(jnp.int32, (B, B), 0) == lax.broadcasted_iota(jnp.int32, (B, B), 1)
        ).astype(F32)
        centre = stacked(m.ac[1])
        m.st[0] = jnp.zeros((B, B), F32)
        m.st[1] = COEF_ONE * m.ac[0] + COEF_TWO * product(centre, beside(m.ac[0]))
        m.st[2] = COEF_ZERO * eye + COEF_ONE * m.ac[1] + COEF_TWO * product(centre, beside(m.ac[1]))
        m.st[3] = COEF_ONE * m.ac[2] + COEF_TWO * product(centre, beside(m.ac[2]))
        m.st[4] = jnp.zeros((B, B), F32)
        for side in range(2):
            @pl.when(has[side])
            def _():
                arrived(m.ahalo.at[side], m.ahalo_recv.at[side])
                edge = stacked(m.ac[2 * side])
                for d in range(3):
                    to = 2 * side + d
                    m.st[to] = m.st[to] + COEF_TWO * product(edge, beside(m.ahalo[side, d]))
        st_own = stacked(m.st[2])
        for i, d in enumerate((0, 1, 3, 4)):
            m.st_far[:, pl.ds(i * B, B)] = stacked(m.st[d])
        for pair in range(2):
            arrived(m.coarse_in.at[pair], m.coarse_recv.at[pair])
        m.cv[...] = m.coarse_in[0] + m.coarse_in[1]
        for i in range(4):
            go(
                lambda i=i: copy(
                    m.cv, m.chalo.at[3 - i], m.chalo_send.at[i], m.chalo_recv.at[3 - i], lvl, row + far[i]
                ),
                has_far[i],
            )
        own = product(st_own, beside(m.cv[...]))
        for i in range(4):
            @pl.when(has_far[i])
            def _():
                arrived(m.chalo.at[i], m.chalo_recv.at[i])
        m.fix[0] = own + product(m.st_far[...], beside(m.chalo[...].reshape(4 * B, B)))
        for to in (5, 4, 6, 3):
            go(
                lambda to=to: copy(
                    m.fix.at[0], m.fix.at[0], m.fix_send.at[0, to], m.fix_recv.at[0], to
                )
            )
        arrived(m.a_buf, m.a_recv)
        go(lambda: copy(m.a_buf, m.a_buf, m.a_send.at[0], m.a_recv, 3))
        hop_up()
        out[pl.ds(0, B)] = jnp.zeros((B, B), F32)
        out[pl.ds(2 * B, B)] = jnp.zeros((B, B), F32)
        arrived(m.fix.at[1], m.fix_recv.at[1])
        out[pl.ds(B, B)] = m.fix[1]
        drain()


def scratch():
    dma = lambda *shape: pltpu.SemaphoreType.DMA(shape)
    block = lambda *lead: pltpu.VMEM(lead + (B, B), F32)
    slab = lambda *lead: pltpu.VMEM(lead + (SLOTS * B, B), F32)
    parts = lambda *lead: pltpu.VMEM(lead + (2 * B, B), BF16)
    return dict(
        rhs=slab(), ops=block(SLOTS * OPT), links=block(SLOTS, 2),
        wide=pltpu.VMEM((3, 2 * SLOTS * B, SLOTS * B), BF16), small=parts(2, 3), link_parts=parts(SLOTS, 2),
        field=slab(5), halo=slab(5, 2), sol=slab(), smooth=slab(),
        rs_src=block(2, 4), rs_in=block(2, 5), sum_src=block(), mid_in=block(2, 2),
        part_src=block(), coarse_in=block(2), fix=block(2), fbuf=block(2, 4),
        t_src=block(2), t_buf=block(4), t_part=parts(4), p_buf=block(4), p_part=parts(4), lift=block(SLOTS), hop_in=block(),
        a_src=block(2, 3), a_buf=block(3), ac=block(3), ahalo=block(2, 3),
        st=block(5), st_far=pltpu.VMEM((2 * B, 4 * B), BF16),
        cv=block(), chalo=block(4), kv=block(2), khalo=block(2, 2), u_src=block(), u_in=block(4),
        mv=block(2), mhalo=block(2, 2), mid_out=block(2),
        in_sem=dma(3), halo_send=dma(5, 2), halo_recv=dma(5, 2),
        rs_send=dma(2, 4), rs_recv=dma(2, 5), sum_send=pltpu.SemaphoreType.DMA, mid_recv=dma(2, 2),
        four_send=dma(8), part_send=pltpu.SemaphoreType.DMA, coarse_recv=dma(2),
        fix_send=dma(2, 8), fix_recv=dma(2), f_send=dma(2, 2), gather_send=dma(2, 4), f_recv=dma(2, 4),
        t_send=dma(4), t_recv=dma(4), p_send=dma(4), p_recv=dma(4), hop_send=dma(5), hop_recv=pltpu.SemaphoreType.DMA,
        a_send=dma(2), a_recv=pltpu.SemaphoreType.DMA, ahalo_send=dma(2), ahalo_recv=dma(2),
        st_send=pltpu.SemaphoreType.DMA, ac_recv=pltpu.SemaphoreType.DMA,
        chalo_send=dma(4), chalo_recv=dma(4), khalo_send=dma(2, 2), khalo_recv=dma(2, 2), u_send=pltpu.SemaphoreType.DMA, u_recv=dma(4),
        mhalo_send=dma(2, 2), mhalo_recv=dma(2, 2), mid_send=pltpu.SemaphoreType.DMA, mid_out_recv=dma(2),
    )


def solution(mesh):
    n_row = mesh.shape["row"]

    def per_device(rhs, op_tiles, op_cols, link_tiles, level_links):
        held = scratch()
        out = pl.pallas_call(
            functools.partial(kernel, n_row, tuple(held)),
            name="multigrid",
            out_shape=jax.ShapeDtypeStruct((SLOTS * B, B), F32),
            in_specs=[
                pl.BlockSpec(memory_space=pl.ANY),
                pl.BlockSpec(memory_space=pl.ANY),
                pl.BlockSpec(memory_space=pltpu.SMEM),
                pl.BlockSpec(memory_space=pl.ANY),
                pl.BlockSpec(memory_space=pltpu.SMEM),
            ],
            out_specs=pl.BlockSpec(memory_space=pltpu.VMEM),
            scratch_shapes=list(held.values()),
            compiler_params=pltpu.CompilerParams(
                collective_id=0, has_side_effects=True, vmem_limit_bytes=60 * 1024 * 1024
            ),
        )(
            rhs.reshape(SLOTS * B, B),
            op_tiles.reshape(SLOTS * OPT, B, B),
            op_cols.transpose(0, 2, 1, 3),
            link_tiles.reshape(SLOTS, 2, B, B),
            level_links.transpose(0, 1, 3, 2),
        )
        return out.reshape(1, 1, SLOTS, B, B)

    placed = (
        P("lvl", "row", None, None, None),
        P("lvl", "row", None, None, None, None),
        P("lvl", "row", None, None),
        P("lvl", "row", None, None, None, None),
        P("lvl", "row", None, None),
    )
    return jax.shard_map(
        per_device,
        mesh=mesh,
        in_specs=placed,
        out_specs=P("lvl", "row", None, None, None),
        check_vma=False,
    )
```

```python
import functools
import types

import jax
import jax.numpy as jnp
from jax import lax
from jax.experimental import pallas as pl
from jax.experimental.pallas import tpu as pltpu
from jax.sharding import PartitionSpec as P

B = 128
SLOTS = 3
OPT = 7
COEF_ZERO = 0.9
COEF_ONE = -0.36
COEF_TWO = 0.05
MESH = pl.DeviceIdType.MESH
F32 = jnp.float32
BF16 = jnp.bfloat16


def halves(value):
    high = value.astype(BF16)
    return high, (value - high.astype(F32)).astype(BF16)


def stacked(value):
    return jnp.concatenate(halves(value), axis=0)


def beside(value):
    return jnp.concatenate(halves(value), axis=1)


def product(left, right):
    full = jnp.dot(left, right, preferred_element_type=F32)
    rows, columns = full.shape[0] // 2, full.shape[1] // 2
    cross = full[:rows, columns:] + full[rows:, :columns]
    return full[:rows, :columns] + (cross + full[rows:, columns:])


def kernel(n_row, names, rhs_hbm, ops_hbm, cols, links_hbm, targets, out, *refs):
    m = types.SimpleNamespace(**dict(zip(names, refs)))
    lvl = lax.axis_index("lvl")
    row = lax.axis_index("row")
    is_fine = lvl < 5
    is_mid = (lvl >= 5) & (lvl < 7)
    is_coarse = lvl == 7
    plane = lvl < 4
    four = lvl == 4
    root = lvl == 0
    has = (row > 0, row < n_row - 1)
    near = (row - 1, row + 1)
    far = (-2, -1, 1, 2)
    has_far = (row > 1, row > 0, row < n_row - 1, row < n_row - 2)

    load_rhs = pltpu.make_async_copy(rhs_hbm, m.rhs, m.in_sem.at[0])
    load_links = pltpu.make_async_copy(links_hbm, m.links, m.in_sem.at[1])
    load_ops = pltpu.make_async_copy(ops_hbm, m.ops, m.in_sem.at[2])
    for load in (load_rhs, load_links, load_ops):
        load.start()

    barrier = pltpu.get_barrier_semaphore()
    for step in range(1, 8):
        pl.semaphore_signal(
            barrier, inc=1, device_id={"lvl": lax.rem(lvl + step, 8), "row": row}, device_id_type=MESH
        )
    for step, there in zip(far, has_far):
        @pl.when(there)
        def _():
            pl.semaphore_signal(
                barrier, inc=1, device_id={"lvl": lvl, "row": row + step}, device_id_type=MESH
            )

    def meet():
        pl.semaphore_wait(barrier, 7 + sum(one.astype(jnp.int32) for one in has_far))

    pending = []

    def go(make, cond=None):
        pending.append((make, cond))
        if cond is None:
            make().start()
        else:
            pl.when(cond)(lambda: make().start())

    def drain():
        for make, cond in pending:
            if cond is None:
                make().wait_send()
            else:
                pl.when(cond)(lambda: make().wait_send())
        pending.clear()

    def copy(src, dst, send, recv, to_lvl, to_row=None):
        return pltpu.make_async_remote_copy(
            src_ref=src, dst_ref=dst, send_sem=send, recv_sem=recv,
            device_id={"lvl": to_lvl, "row": row if to_row is None else to_row},
            device_id_type=MESH,
        )

    def arrived(ref, sem):
        pltpu.make_async_copy(ref, ref, sem).wait()

    def out_copy(src, slot):
        return pltpu.make_async_copy(src, out.at[pl.ds(slot * B, B)], m.out_sem.at[slot])

    def store(src, slot):
        out_copy(src, slot).start()

    def stored(slot):
        out_copy(m.res.at[pl.ds(slot * B, B)], slot).wait()

    def halo_go(turn, src, rows, cond=True):
        part = pl.ds(0, rows)
        for side in range(2):
            go(
                lambda side=side: copy(
                    src.at[part], m.halo.at[turn, 1 - side, part],
                    m.halo_send.at[turn, side], m.halo_recv.at[turn, 1 - side], lvl, near[side],
                ),
                has[side] & cond,
            )

    def halo_arrived(turn, side, rows):
        arrived(m.halo.at[turn, side, pl.ds(0, rows)], m.halo_recv.at[turn, side])

    def code_of(s, j):
        return cols[0, s, 0, j]

    def gathered_tile(s, code):
        total = jnp.zeros((B, B), F32)
        for j in range(OPT):
            total = total + jnp.where(code_of(s, j) == code, F32(1), F32(0)) * m.ops[s * OPT + j]
        return total

    def clear_missing(ref, conditions):
        for i, there in enumerate(conditions):
            @pl.when(jnp.logical_not(there))
            def _():
                ref[i] = jnp.zeros((B, B), F32)

    def side_go(turn, src, halo, send, recv, cond):
        for side in range(2):
            go(
                lambda side=side: copy(
                    src.at[turn], halo.at[turn, 1 - side],
                    send.at[turn, side], recv.at[turn, 1 - side], lvl, near[side],
                ),
                has[side] & cond,
            )

    def side_image(turn, parts, src, halo, recv):
        own = product(parts(1), beside(src[turn]))
        for side in range(2):
            @pl.when(has[side])
            def _():
                arrived(halo.at[turn, side], recv.at[turn, side])
        for side in range(2):
            own = own + product(parts(2 * side), beside(halo[turn, side]))
        return own

    @pl.when(is_fine)
    def _():
        load_links.wait()
        for s in range(SLOTS):
            for kind in range(2):
                m.link_parts[s, kind] = stacked(m.links[s, kind])
        load_rhs.wait()

        def restrict(cycle, resid_of):
            terms = [
                product(m.link_parts[s, 0], beside(resid_of(s))) for s in range(SLOTS)
            ]
            for k in range(4):
                total = jnp.zeros((B, B), F32)
                for s in range(SLOTS):
                    hit = jnp.where(targets[0, 0, 0, s] == k, F32(1), F32(0))
                    total = total + hit * terms[s]
                m.rs_src[cycle, k] = total
            return terms

        def send_terms(cycle):
            for step in range(1, 4):
                to = lax.rem(lvl + step, 4)
                go(
                    lambda step=step, to=to: copy(
                        m.rs_src.at[cycle, to], m.rs_in.at[cycle, lvl],
                        m.rs_send.at[cycle, step], m.rs_recv.at[cycle, lvl], to,
                    ),
                    plane,
                )

        def plane_sum(cycle):
            total = m.rs_src[cycle, lvl]
            for step in range(1, 4):
                source = lax.rem(lvl + step, 4)
                arrived(m.rs_in.at[cycle, source], m.rs_recv.at[cycle, source])
                total = total + m.rs_in[cycle, source]
            return total

        def gather_go(cycle):
            for step in range(1, 4):
                go(
                    lambda step=step: copy(
                        m.fbuf.at[cycle, lvl], m.fbuf.at[cycle, lvl],
                        m.gather_send.at[cycle, step], m.f_recv.at[cycle, lvl], lax.rem(lvl + step, 4),
                    ),
                    plane,
                )

        def image(turn, src, dst):
            dst[...] = product(m.wide[1], beside(src[...]))
            for side in range(2):
                @pl.when(has[side])
                def _():
                    halo_arrived(turn, side, SLOTS * B)
                    dst[...] = dst[...] + product(m.wide[2 * side], beside(m.halo[turn, side]))

        def raise_fix(cycle):
            coarse = beside(m.fix[cycle])
            for s in range(SLOTS):
                m.lift[s] = m.fix[cycle] + product(m.p_part[targets[0, 0, 1, s]], coarse)

        def correct(cycle, dest):
            for s in range(SLOTS):
                chosen = m.lift[s] + m.fbuf[cycle, targets[0, 0, 1, s]]
                rows = pl.ds(s * B, B)
                dest[rows] = m.smooth[rows] + product(m.link_parts[s, 1], beside(chosen))
                if cycle == 1:
                    store(dest.at[rows], s)

        def blend(resid, first):
            return COEF_ZERO * resid[...] + COEF_ONE * first[...] + COEF_TWO * m.smooth[...]

        restrict(0, lambda s: m.rhs[pl.ds(s * B, B)])
        meet()
        send_terms(0)
        for k in range(4):
            go(
                lambda k=k: copy(
                    m.rs_src.at[0, k], m.mid_in.at[k % 2, 1],
                    m.four_send.at[k], m.mid_recv.at[k % 2, 1], 5 + k // 2,
                ),
                four,
            )
        halo_go(0, m.rhs, SLOTS * B)

        load_ops.wait()

        def dense(s, carry):
            for code in range(3 * SLOTS):
                high, low = halves(gathered_tile(s, code))
                columns = pl.ds((code % SLOTS) * B, B)
                m.wide[code // SLOTS, pl.ds(pl.multiple_of(s * B, B), B), columns] = high
                m.wide[code // SLOTS, pl.ds(pl.multiple_of((SLOTS + s) * B, B), B), columns] = low
            return carry

        lax.fori_loop(0, SLOTS, dense, 0)

        sum_copy = lambda: copy(
            m.sum_src, m.mid_in.at[lax.rem(lvl, 2), 0],
            m.sum_send, m.mid_recv.at[lax.rem(lvl, 2), 0], 5 + lvl // 2,
        )

        @pl.when(plane)
        def _():
            m.sum_src[...] = plane_sum(0)
            sum_copy().start()

        first = m.field.at[1]
        image(0, m.rhs, first)

        @pl.when(plane)
        def _():
            sum_copy().wait_send()

        @pl.when(four)
        def _():
            arrived(m.p_buf.at[0], m.p_recv.at[0])

        go(lambda: copy(m.p_buf.at[0], m.p_buf.at[0], m.hop_send.at[0], m.p_recv.at[0], 0), four)
        halo_go(1, first, SLOTS * B)
        image(1, first, m.smooth)
        m.smooth[...] = blend(m.rhs, first)

        def spread_tile(buf, send, recv):
            @pl.when(plane)
            def _():
                arrived(buf.at[lvl], recv.at[lvl])

            for step in range(1, 4):
                go(
                    lambda step=step: copy(
                        buf.at[lvl], buf.at[lvl], send.at[step], recv.at[lvl], lax.rem(lvl + step, 4)
                    ),
                    plane,
                )

        spread_tile(m.p_buf, m.p_send, m.p_recv)

        @pl.when(four)
        def _():
            arrived(m.a_buf, m.a_recv)

        go(lambda: copy(m.a_buf, m.a_buf, m.hop_send.at[2], m.a_recv, 0), four)

        @pl.when(root)
        def _():
            clear_missing(m.khalo.at[0], has)
            clear_missing(m.khalo.at[1], has)

        @pl.when(plane)
        def _():
            clear_missing(m.mhalo.at[0], has)
            clear_missing(m.mhalo.at[1], has)
            arrived(m.fbuf.at[0, lvl], m.f_recv.at[0, lvl])

        gather_go(0)

        @pl.when(plane)
        def _():
            for step in range(1, 4):
                source = lax.rem(lvl + step, 4)
                arrived(m.p_buf.at[source], m.p_recv.at[source])

        @pl.when(four)
        def _():
            for k in range(1, 4):
                arrived(m.p_buf.at[k], m.p_recv.at[k])

        for k in range(4):
            m.p_part[k] = stacked(m.p_buf[k])

        arrived(m.fix.at[0], m.fix_recv.at[0])
        go(lambda: copy(m.fix.at[0], m.fix.at[0], m.hop_send.at[4], m.fix_recv.at[0], 0), four)
        raise_fix(0)
        spread_tile(m.t_buf, m.t_send, m.t_recv)

        @pl.when(plane)
        def _():
            for step in range(1, 4):
                source = lax.rem(lvl + step, 4)
                arrived(m.fbuf.at[0, source], m.f_recv.at[0, source])

        @pl.when(four)
        def _():
            for k in range(4):
                arrived(m.fbuf.at[0, k], m.f_recv.at[0, k])

        correct(0, m.sol)

        halo_go(2, m.sol, SLOTS * B)

        image(2, m.sol, m.smooth)
        resid = m.field.at[3]
        resid[...] = m.rhs[...] - m.smooth[...]
        halo_go(3, resid, SLOTS * B, plane)
        terms = restrict(1, lambda s: m.field[3, pl.ds(s * B, B)])
        send_terms(1)
        for k in range(1, 4):
            go(
                lambda k=k: copy(m.rs_src.at[1, k], m.hop_in, m.four_send.at[4 + k], m.hop_recv, 4 + k),
                four,
            )
        @pl.when(plane)
        def _():
            for step in range(1, 4):
                source = lax.rem(lvl + step, 4)
                arrived(m.t_buf.at[source], m.t_recv.at[source])

        @pl.when(four)
        def _():
            for k in range(4):
                arrived(m.t_buf.at[k], m.t_recv.at[k])

        for k in range(4):
            m.t_part[k] = stacked(m.t_buf[k])

        total = jnp.zeros((B, B), F32)
        for s in range(SLOTS):
            total = total + product(m.t_part[targets[0, 0, 0, s]], beside(terms[s]))
        m.u_src[...] = total
        slot = jnp.maximum(lvl - 1, 0)
        go(
            lambda: copy(m.u_src, m.u_in.at[slot], m.u_send, m.u_recv.at[slot], 0),
            jnp.logical_not(root),
        )
        go(
            lambda: copy(m.rs_src.at[1, 0], m.rs_in.at[1, 4], m.four_send.at[4], m.rs_recv.at[1, 4], 0),
            four,
        )
        halo_go(3, resid, SLOTS * B, four)

        mid_sides = (m.mv, m.mhalo, m.mhalo_send, m.mhalo_recv)
        top_sides = (m.kv, m.khalo, m.khalo_send, m.khalo_recv)

        def mid_image(turn):
            return side_image(turn, lambda d: m.small[0, d], m.mv, m.mhalo, m.mhalo_recv)

        def top_image(turn):
            return side_image(turn, lambda d: m.small[1, d], m.kv, m.khalo, m.khalo_recv)

        @pl.when(plane)
        def _():
            total = plane_sum(1)
            arrived(m.rs_in.at[1, 4], m.rs_recv.at[1, 4])
            m.mv[0] = total + m.rs_in[1, 4]

        side_go(0, *mid_sides, plane)

        @pl.when(root)
        def _():
            total = m.u_src[...]
            for i in range(4):
                arrived(m.u_in.at[i], m.u_recv.at[i])
                total = total + m.u_in[i]
            m.kv[0] = total

        side_go(0, *top_sides, root)

        @pl.when(plane)
        def _():
            arrived(m.a_buf, m.a_recv)
            for d in range(3):
                m.small[0, d] = stacked(m.a_buf[d])

        @pl.when(root)
        def _():
            arrived(m.ac, m.ac_recv)
            for d in range(3):
                m.small[1, d] = stacked(m.ac[d])

        first = m.field.at[4]
        image(3, resid, first)

        @pl.when(plane)
        def _():
            m.mv[1] = mid_image(0)

        side_go(1, *mid_sides, plane)

        @pl.when(root)
        def _():
            m.kv[1] = top_image(0)

        side_go(1, *top_sides, root)
        halo_go(4, first, SLOTS * B)

        @pl.when(plane)
        def _():
            m.fbuf[1, lvl] = COEF_ZERO * m.mv[0] + COEF_ONE * m.mv[1] + COEF_TWO * mid_image(1)

        gather_go(1)
        go(
            lambda: copy(m.fbuf.at[1, lvl], m.fbuf.at[1, lvl], m.f_send.at[0, 0], m.f_recv.at[1, lvl], 4),
            plane,
        )
        go(
            lambda: copy(
                m.fbuf.at[1, lvl], m.mid_out.at[lax.rem(lvl, 2)], m.mid_send, m.mid_out_recv.at[lax.rem(lvl, 2)],
                5 + lvl // 2,
            ),
            plane & jnp.logical_not(root),
        )
        @pl.when(root)
        def _():
            m.fix[1] = COEF_ZERO * m.kv[0] + COEF_ONE * m.kv[1] + COEF_TWO * top_image(1)

        for to in (4, 2, 1, 3):
            go(
                lambda to=to: copy(
                    m.fix.at[1], m.fix.at[1], m.fix_send.at[1, to], m.fix_recv.at[1], to
                ),
                root,
            )

        image(4, first, m.smooth)
        m.smooth[...] = m.sol[...] + blend(resid, first)

        @pl.when(four)
        def _():
            arrived(m.fbuf.at[1, 0], m.f_recv.at[1, 0])

        go(lambda: copy(m.fbuf.at[1, 0], m.mid_out.at[0], m.mid_send, m.mid_out_recv.at[0], 5), four)

        @pl.when(jnp.logical_not(root))
        def _():
            arrived(m.fix.at[1], m.fix_recv.at[1])

        go(
            lambda: copy(m.fix.at[1], m.fix.at[1], m.fix_send.at[1, 5], m.fix_recv.at[1], lvl + 4),
            plane & jnp.logical_not(root),
        )
        raise_fix(1)

        @pl.when(plane)
        def _():
            for step in range(1, 4):
                source = lax.rem(lvl + step, 4)
                arrived(m.fbuf.at[1, source], m.f_recv.at[1, source])

        @pl.when(four)
        def _():
            for k in range(1, 4):
                arrived(m.fbuf.at[1, k], m.f_recv.at[1, k])

        correct(1, m.res)
        drain()
        for slot in range(SLOTS):
            stored(slot)

    def hop_up():
        arrived(m.hop_in, m.hop_recv)
        go(lambda: copy(m.hop_in, m.rs_in.at[1, 4], m.hop_send.at[1], m.rs_recv.at[1, 4], lvl - 4))

    @pl.when(is_mid)
    def _():
        pair = lvl - 5
        m.res[pl.ds(B, B)] = jnp.zeros((B, B), F32)
        store(m.res.at[pl.ds(B, B)], 1)
        load_links.wait()
        eye = (
            lax.broadcasted_iota(jnp.int32, (B, B), 0) == lax.broadcasted_iota(jnp.int32, (B, B), 1)
        ).astype(F32)
        for p in range(2):
            tile = m.links[2 * p, 0] + 0.5 * eye
            m.t_src[p] = tile
            m.link_parts[2 * p, 0] = stacked(tile)
            m.link_parts[2 * p, 1] = stacked(m.links[2 * p, 1])
        load_rhs.wait()
        meet()
        def smooth_go(p, way, to):
            k = 2 * pair + p
            go(lambda: copy(m.fbuf.at[0, k], m.fbuf.at[0, k], m.f_send.at[p, way], m.f_recv.at[0, k], to))

        def ship(src, dst, recv, send, k):
            go(lambda: copy(src, dst, send.at[0], recv, 4))
            go(lambda: copy(src, dst, send.at[1], recv, k), k > 0)

        for p in range(2):
            k = 2 * pair + p
            ship(m.links.at[2 * p, 1], m.p_buf.at[k], m.p_recv.at[k], m.p_send.at[pl.ds(2 * p, 2)], k)
        load_ops.wait()
        for p in range(2):
            for d in range(3):
                tile = gathered_tile(2 * p, d * SLOTS + 2 * p)
                m.a_src[p, d] = tile
                m.small[p, d] = stacked(tile)
        for p in range(2):
            k = 2 * pair + p
            to = k + 4 * (1 - (lax.rem(k, 3) + 1) // 2)
            go(lambda p=p, to=to: copy(m.a_src.at[p], m.a_buf, m.a_send.at[p], m.a_recv, to))
        for p in range(2):
            k = 2 * pair + p
            go(
                lambda p=p, k=k: copy(
                    m.t_src.at[p], m.t_buf.at[k], m.t_send.at[p], m.t_recv.at[k], k
                )
            )

        def level_image(turn, dst):
            for p in range(2):
                part = pl.ds(p * B, B)
                dst[part] = product(m.small[p, 1], beside(m.field[turn, part]))
            for side in range(2):
                @pl.when(has[side])
                def _():
                    halo_arrived(turn, side, 2 * B)
                    for p in range(2):
                        part = pl.ds(p * B, B)
                        dst[part] = dst[part] + product(
                            m.small[p, 2 * side], beside(m.halo[turn, side, part])
                        )

        for p in range(2):
            for source in (1, 0):
                arrived(m.mid_in.at[p, source], m.mid_recv.at[p, source])
            m.field[0, pl.ds(p * B, B)] = m.mid_in[p, 0] + m.mid_in[p, 1]
        total = product(m.link_parts[0, 0], beside(m.field[0, pl.ds(0, B)]))
        m.part_src[...] = total + product(m.link_parts[2, 0], beside(m.field[0, pl.ds(B, B)]))
        go(lambda: copy(m.part_src, m.coarse_in.at[pair], m.part_send, m.coarse_recv.at[pair], 7))
        halo_go(0, m.field.at[0], 2 * B)
        level_image(0, m.field.at[1])
        halo_go(1, m.field.at[1], 2 * B)
        level_image(1, m.smooth)
        part = pl.ds(0, 2 * B)
        m.smooth[part] = (
            COEF_ZERO * m.field[0, part] + COEF_ONE * m.field[1, part] + COEF_TWO * m.smooth[part]
        )
        for p in range(2):
            k = 2 * pair + p
            m.fbuf[0, k] = m.smooth[pl.ds(p * B, B)]
            smooth_go(p, 0, k)
        for p in range(2):
            smooth_go(p, 1, 4)
        arrived(m.fix.at[0], m.fix_recv.at[0])
        go(lambda: copy(m.fix.at[0], m.fix.at[0], m.hop_send.at[0], m.fix_recv.at[0], lvl - 4))
        for p in range(2):
            k = 2 * pair + p
            go(lambda p=p, k=k: copy(m.t_src.at[p], m.t_buf.at[k], m.t_send.at[2 + p], m.t_recv.at[k], 4))
        hop_up()
        arrived(m.fix.at[1], m.fix_recv.at[1])
        for p in range(2):
            m.lift[p] = product(m.link_parts[2 * p, 1], beside(m.fix[1]))
        for p in range(2):
            arrived(m.mid_out.at[p], m.mid_out_recv.at[p])
            rows = pl.ds(2 * p * B, B)
            m.res[rows] = m.mid_out[p] + m.lift[p]
            store(m.res.at[rows], 2 * p)
        drain()
        for slot in range(SLOTS):
            stored(slot)

    @pl.when(is_coarse)
    def _():
        m.res[...] = jnp.zeros((SLOTS * B, B), F32)
        for slot in (0, 2):
            store(m.res.at[pl.ds(slot * B, B)], slot)
        load_links.wait()
        load_rhs.wait()
        load_ops.wait()
        for d in range(3):
            m.ac[d] = gathered_tile(1, d * SLOTS + 1)
        clear_missing(m.chalo, has_far)
        meet()
        for side in range(2):
            go(
                lambda side=side: copy(
                    m.ac, m.ahalo.at[1 - side], m.ahalo_send.at[side], m.ahalo_recv.at[1 - side], lvl, near[side]
                ),
                has[side],
            )
        go(lambda: copy(m.ac, m.ac, m.st_send, m.ac_recv, 0))
        eye = (
            lax.broadcasted_iota(jnp.int32, (B, B), 0) == lax.broadcasted_iota(jnp.int32, (B, B), 1)
        ).astype(F32)
        centre = stacked(m.ac[1])
        m.st[0] = jnp.zeros((B, B), F32)
        m.st[1] = COEF_ONE * m.ac[0] + COEF_TWO * product(centre, beside(m.ac[0]))
        m.st[2] = COEF_ZERO * eye + COEF_ONE * m.ac[1] + COEF_TWO * product(centre, beside(m.ac[1]))
        m.st[3] = COEF_ONE * m.ac[2] + COEF_TWO * product(centre, beside(m.ac[2]))
        m.st[4] = jnp.zeros((B, B), F32)
        for side in range(2):
            @pl.when(has[side])
            def _():
                arrived(m.ahalo.at[side], m.ahalo_recv.at[side])
                edge = stacked(m.ac[2 * side])
                for d in range(3):
                    to = 2 * side + d
                    m.st[to] = m.st[to] + COEF_TWO * product(edge, beside(m.ahalo[side, d]))
        st_own = stacked(m.st[2])
        for i, d in enumerate((0, 1, 3, 4)):
            m.st_far[:, pl.ds(i * B, B)] = stacked(m.st[d])
        for pair in range(2):
            arrived(m.coarse_in.at[pair], m.coarse_recv.at[pair])
        m.cv[...] = m.coarse_in[0] + m.coarse_in[1]
        for i in range(4):
            go(
                lambda i=i: copy(
                    m.cv, m.chalo.at[3 - i], m.chalo_send.at[i], m.chalo_recv.at[3 - i], lvl, row + far[i]
                ),
                has_far[i],
            )
        own = product(st_own, beside(m.cv[...]))
        for i in range(4):
            @pl.when(has_far[i])
            def _():
                arrived(m.chalo.at[i], m.chalo_recv.at[i])
        m.fix[0] = own + product(m.st_far[...], beside(m.chalo[...].reshape(4 * B, B)))
        for to in (5, 4, 6, 3):
            go(
                lambda to=to: copy(
                    m.fix.at[0], m.fix.at[0], m.fix_send.at[0, to], m.fix_recv.at[0], to
                )
            )
        arrived(m.a_buf, m.a_recv)
        go(lambda: copy(m.a_buf, m.a_buf, m.a_send.at[0], m.a_recv, 3))
        hop_up()
        arrived(m.fix.at[1], m.fix_recv.at[1])
        store(m.fix.at[1], 1)
        drain()
        for slot in range(SLOTS):
            stored(slot)


def scratch():
    dma = lambda *shape: pltpu.SemaphoreType.DMA(shape)
    block = lambda *lead: pltpu.VMEM(lead + (B, B), F32)
    slab = lambda *lead: pltpu.VMEM(lead + (SLOTS * B, B), F32)
    parts = lambda *lead: pltpu.VMEM(lead + (2 * B, B), BF16)
    return dict(
        rhs=slab(), ops=block(SLOTS * OPT), links=block(SLOTS, 2),
        wide=pltpu.VMEM((3, 2 * SLOTS * B, SLOTS * B), BF16), small=parts(2, 3), link_parts=parts(SLOTS, 2),
        field=slab(5), halo=slab(5, 2), sol=slab(), smooth=slab(),
        rs_src=block(2, 4), rs_in=block(2, 5), sum_src=block(), mid_in=block(2, 2),
        part_src=block(), coarse_in=block(2), fix=block(2), fbuf=block(2, 4),
        t_src=block(2), t_buf=block(4), t_part=parts(4), p_buf=block(4), p_part=parts(4), lift=block(SLOTS), hop_in=block(), res=slab(),
        a_src=block(2, 3), a_buf=block(3), ac=block(3), ahalo=block(2, 3),
        st=block(5), st_far=pltpu.VMEM((2 * B, 4 * B), BF16),
        cv=block(), chalo=block(4), kv=block(2), khalo=block(2, 2), u_src=block(), u_in=block(4),
        mv=block(2), mhalo=block(2, 2), mid_out=block(2),
        in_sem=dma(3), out_sem=dma(SLOTS), halo_send=dma(5, 2), halo_recv=dma(5, 2),
        rs_send=dma(2, 4), rs_recv=dma(2, 5), sum_send=pltpu.SemaphoreType.DMA, mid_recv=dma(2, 2),
        four_send=dma(8), part_send=pltpu.SemaphoreType.DMA, coarse_recv=dma(2),
        fix_send=dma(2, 8), fix_recv=dma(2), f_send=dma(2, 2), gather_send=dma(2, 4), f_recv=dma(2, 4),
        t_send=dma(4), t_recv=dma(4), p_send=dma(4), p_recv=dma(4), hop_send=dma(5), hop_recv=pltpu.SemaphoreType.DMA,
        a_send=dma(2), a_recv=pltpu.SemaphoreType.DMA, ahalo_send=dma(2), ahalo_recv=dma(2),
        st_send=pltpu.SemaphoreType.DMA, ac_recv=pltpu.SemaphoreType.DMA,
        chalo_send=dma(4), chalo_recv=dma(4), khalo_send=dma(2, 2), khalo_recv=dma(2, 2), u_send=pltpu.SemaphoreType.DMA, u_recv=dma(4),
        mhalo_send=dma(2, 2), mhalo_recv=dma(2, 2), mid_send=pltpu.SemaphoreType.DMA, mid_out_recv=dma(2),
    )


def solution(mesh):
    n_row = mesh.shape["row"]

    def per_device(rhs, op_tiles, op_cols, link_tiles, level_links):
        held = scratch()
        out = pl.pallas_call(
            functools.partial(kernel, n_row, tuple(held)),
            name="multigrid",
            out_shape=jax.ShapeDtypeStruct((SLOTS * B, B), F32),
            in_specs=[
                pl.BlockSpec(memory_space=pl.ANY),
                pl.BlockSpec(memory_space=pl.ANY),
                pl.BlockSpec(memory_space=pltpu.SMEM),
                pl.BlockSpec(memory_space=pl.ANY),
                pl.BlockSpec(memory_space=pltpu.SMEM),
            ],
            out_specs=pl.BlockSpec(memory_space=pl.ANY),
            scratch_shapes=list(held.values()),
            compiler_params=pltpu.CompilerParams(
                collective_id=0, has_side_effects=True, vmem_limit_bytes=60 * 1024 * 1024
            ),
        )(
            rhs.reshape(SLOTS * B, B),
            op_tiles.reshape(SLOTS * OPT, B, B),
            op_cols.transpose(0, 2, 1, 3),
            link_tiles.reshape(SLOTS, 2, B, B),
            level_links.transpose(0, 1, 3, 2),
        )
        return out.reshape(1, 1, SLOTS, B, B)

    placed = (
        P("lvl", "row", None, None, None),
        P("lvl", "row", None, None, None, None),
        P("lvl", "row", None, None),
        P("lvl", "row", None, None, None, None),
        P("lvl", "row", None, None),
    )
    return jax.shard_map(
        per_device,
        mesh=mesh,
        in_specs=placed,
        out_specs=P("lvl", "row", None, None, None),
        check_vma=False,
    )
```

```python
import functools
import types

import jax
import jax.numpy as jnp
from jax import lax
from jax.experimental import pallas as pl
from jax.experimental.pallas import tpu as pltpu
from jax.sharding import PartitionSpec as P

B = 128
SLOTS = 3
OPT = 7
COEF_ZERO = 0.9
COEF_ONE = -0.36
COEF_TWO = 0.05
MESH = pl.DeviceIdType.MESH
F32 = jnp.float32
BF16 = jnp.bfloat16


def halves(value):
    high = value.astype(BF16)
    return high, (value - high.astype(F32)).astype(BF16)


def stacked(value):
    return jnp.concatenate(halves(value), axis=0)


def beside(value):
    return jnp.concatenate(halves(value), axis=1)


def product(left, right):
    full = jnp.dot(left, right, preferred_element_type=F32)
    rows, columns = full.shape[0] // 2, full.shape[1] // 2
    cross = full[:rows, columns:] + full[rows:, :columns]
    return full[:rows, :columns] + (cross + full[rows:, columns:])


def kernel(n_row, names, rhs_hbm, ops_hbm, cols, links_hbm, targets, out, *refs):
    m = types.SimpleNamespace(**dict(zip(names, refs)))
    lvl = lax.axis_index("lvl")
    row = lax.axis_index("row")
    is_fine = lvl < 5
    is_mid = (lvl >= 5) & (lvl < 7)
    is_coarse = lvl == 7
    plane = lvl < 4
    four = lvl == 4
    root = lvl == 0
    has = (row > 0, row < n_row - 1)
    near = (row - 1, row + 1)
    far = (-2, -1, 1, 2)
    has_far = (row > 1, row > 0, row < n_row - 1, row < n_row - 2)

    load_rhs = pltpu.make_async_copy(rhs_hbm, m.rhs, m.in_sem.at[0])
    load_links = pltpu.make_async_copy(links_hbm, m.links, m.in_sem.at[1])
    load_ops = pltpu.make_async_copy(ops_hbm, m.ops, m.in_sem.at[2])
    for load in (load_rhs, load_links, load_ops):
        load.start()

    barrier = pltpu.get_barrier_semaphore()
    for step in range(1, 8):
        pl.semaphore_signal(
            barrier, inc=1, device_id={"lvl": lax.rem(lvl + step, 8), "row": row}, device_id_type=MESH
        )
    for step, there in zip(far, has_far):
        @pl.when(there)
        def _():
            pl.semaphore_signal(
                barrier, inc=1, device_id={"lvl": lvl, "row": row + step}, device_id_type=MESH
            )

    def meet():
        pl.semaphore_wait(barrier, 7 + sum(one.astype(jnp.int32) for one in has_far))

    pending = []

    def go(make, cond=None):
        pending.append((make, cond))
        if cond is None:
            make().start()
        else:
            pl.when(cond)(lambda: make().start())

    def drain():
        for make, cond in pending:
            if cond is None:
                make().wait_send()
            else:
                pl.when(cond)(lambda: make().wait_send())
        pending.clear()

    def copy(src, dst, send, recv, to_lvl, to_row=None):
        return pltpu.make_async_remote_copy(
            src_ref=src, dst_ref=dst, send_sem=send, recv_sem=recv,
            device_id={"lvl": to_lvl, "row": row if to_row is None else to_row},
            device_id_type=MESH,
        )

    def arrived(ref, sem):
        pltpu.make_async_copy(ref, ref, sem).wait()

    def out_copy(src, slot):
        return pltpu.make_async_copy(src, out.at[pl.ds(slot * B, B)], m.out_sem.at[slot])

    def store(src, slot):
        out_copy(src, slot).start()

    def stored(slot):
        out_copy(m.res.at[pl.ds(slot * B, B)], slot).wait()

    def halo_go(turn, src, rows, cond=True):
        part = pl.ds(0, rows)
        for side in range(2):
            go(
                lambda side=side: copy(
                    src.at[part], m.halo.at[turn, 1 - side, part],
                    m.halo_send.at[turn, side], m.halo_recv.at[turn, 1 - side], lvl, near[side],
                ),
                has[side] & cond,
            )

    def halo_arrived(turn, side, rows):
        arrived(m.halo.at[turn, side, pl.ds(0, rows)], m.halo_recv.at[turn, side])

    def code_of(s, j):
        return cols[0, s, 0, j]

    def gathered_tile(s, code):
        total = jnp.zeros((B, B), F32)
        for j in range(OPT):
            total = total + jnp.where(code_of(s, j) == code, F32(1), F32(0)) * m.ops[s * OPT + j]
        return total

    def clear_missing(ref, conditions):
        for i, there in enumerate(conditions):
            @pl.when(jnp.logical_not(there))
            def _():
                ref[i] = jnp.zeros((B, B), F32)

    def side_go(turn, src, halo, send, recv, cond):
        for side in range(2):
            go(
                lambda side=side: copy(
                    src.at[turn], halo.at[turn, 1 - side],
                    send.at[turn, side], recv.at[turn, 1 - side], lvl, near[side],
                ),
                has[side] & cond,
            )

    def side_image(turn, parts, src, halo, recv):
        own = product(parts(1), beside(src[turn]))
        for side in range(2):
            @pl.when(has[side])
            def _():
                arrived(halo.at[turn, side], recv.at[turn, side])
        for side in range(2):
            own = own + product(parts(2 * side), beside(halo[turn, side]))
        return own

    @pl.when(is_fine)
    def _():
        load_links.wait()
        for s in range(SLOTS):
            for kind in range(2):
                m.link_parts[s, kind] = stacked(m.links[s, kind])
        load_rhs.wait()

        def restrict(cycle, resid_of):
            terms = [
                product(m.link_parts[s, 0], beside(resid_of(s))) for s in range(SLOTS)
            ]
            for k in range(4):
                total = jnp.zeros((B, B), F32)
                for s in range(SLOTS):
                    hit = jnp.where(targets[0, 0, 0, s] == k, F32(1), F32(0))
                    total = total + hit * terms[s]
                m.rs_src[cycle, k] = total
            return terms

        def send_terms(cycle):
            for step in range(1, 4):
                to = lax.rem(lvl + step, 4)
                go(
                    lambda step=step, to=to: copy(
                        m.rs_src.at[cycle, to], m.rs_in.at[cycle, lvl],
                        m.rs_send.at[cycle, step], m.rs_recv.at[cycle, lvl], to,
                    ),
                    plane,
                )

        def plane_sum(cycle):
            total = m.rs_src[cycle, lvl]
            for step in range(1, 4):
                source = lax.rem(lvl + step, 4)
                arrived(m.rs_in.at[cycle, source], m.rs_recv.at[cycle, source])
                total = total + m.rs_in[cycle, source]
            return total

        def gather_go(cycle):
            for step in range(1, 4):
                go(
                    lambda step=step: copy(
                        m.fbuf.at[cycle, lvl], m.fbuf.at[cycle, lvl],
                        m.gather_send.at[cycle, step], m.f_recv.at[cycle, lvl], lax.rem(lvl + step, 4),
                    ),
                    plane,
                )

        def image(turn, src, dst):
            dst[...] = product(m.wide[1], beside(src[...]))
            for side in range(2):
                @pl.when(has[side])
                def _():
                    halo_arrived(turn, side, SLOTS * B)
                    dst[...] = dst[...] + product(m.wide[2 * side], beside(m.halo[turn, side]))

        def raise_fix(cycle):
            coarse = beside(m.fix[cycle])
            for s in range(SLOTS):
                m.lift[s] = m.fix[cycle] + product(m.p_part[targets[0, 0, 1, s]], coarse)

        def correct(cycle, dest):
            for s in range(SLOTS):
                chosen = m.lift[s] + m.fbuf[cycle, targets[0, 0, 1, s]]
                rows = pl.ds(s * B, B)
                dest[rows] = m.smooth[rows] + product(m.link_parts[s, 1], beside(chosen))
                if cycle == 1:
                    store(dest.at[rows], s)

        def blend(resid, first):
            return COEF_ZERO * resid[...] + COEF_ONE * first[...] + COEF_TWO * m.smooth[...]

        restrict(0, lambda s: m.rhs[pl.ds(s * B, B)])
        meet()
        send_terms(0)
        for k in range(4):
            go(
                lambda k=k: copy(
                    m.rs_src.at[0, k], m.mid_in.at[k % 2, 1],
                    m.four_send.at[k], m.mid_recv.at[k % 2, 1], 5 + k // 2,
                ),
                four,
            )
        halo_go(0, m.rhs, SLOTS * B)

        load_ops.wait()

        def dense(s, carry):
            for code in range(3 * SLOTS):
                high, low = halves(gathered_tile(s, code))
                columns = pl.ds((code % SLOTS) * B, B)
                m.wide[code // SLOTS, pl.ds(pl.multiple_of(s * B, B), B), columns] = high
                m.wide[code // SLOTS, pl.ds(pl.multiple_of((SLOTS + s) * B, B), B), columns] = low
            return carry

        lax.fori_loop(0, SLOTS, dense, 0)

        sum_copy = lambda: copy(
            m.sum_src, m.mid_in.at[lax.rem(lvl, 2), 0],
            m.sum_send, m.mid_recv.at[lax.rem(lvl, 2), 0], 5 + lvl // 2,
        )

        @pl.when(plane)
        def _():
            m.sum_src[...] = plane_sum(0)
            sum_copy().start()

        first = m.field.at[1]
        image(0, m.rhs, first)

        @pl.when(plane)
        def _():
            sum_copy().wait_send()

        @pl.when(four)
        def _():
            arrived(m.p_buf.at[0], m.p_recv.at[0])

        go(lambda: copy(m.p_buf.at[0], m.p_buf.at[0], m.hop_send.at[0], m.p_recv.at[0], 0), four)
        halo_go(1, first, SLOTS * B)
        image(1, first, m.smooth)
        m.smooth[...] = blend(m.rhs, first)

        def spread_tile(buf, send, recv):
            @pl.when(plane)
            def _():
                arrived(buf.at[lvl], recv.at[lvl])

            for step in range(1, 4):
                go(
                    lambda step=step: copy(
                        buf.at[lvl], buf.at[lvl], send.at[step], recv.at[lvl], lax.rem(lvl + step, 4)
                    ),
                    plane,
                )

        spread_tile(m.p_buf, m.p_send, m.p_recv)

        @pl.when(four)
        def _():
            arrived(m.a_buf, m.a_recv)

        go(lambda: copy(m.a_buf, m.a_buf, m.hop_send.at[2], m.a_recv, 0), four)

        @pl.when(root)
        def _():
            clear_missing(m.khalo.at[0], has)
            clear_missing(m.khalo.at[1], has)

        @pl.when(plane)
        def _():
            clear_missing(m.mhalo.at[0], has)
            clear_missing(m.mhalo.at[1], has)
            arrived(m.fbuf.at[0, lvl], m.f_recv.at[0, lvl])

        gather_go(0)

        @pl.when(plane)
        def _():
            for step in range(1, 4):
                source = lax.rem(lvl + step, 4)
                arrived(m.p_buf.at[source], m.p_recv.at[source])

        @pl.when(four)
        def _():
            for k in range(1, 4):
                arrived(m.p_buf.at[k], m.p_recv.at[k])

        for k in range(4):
            m.p_part[k] = stacked(m.p_buf[k])

        arrived(m.fix.at[0], m.fix_recv.at[0])
        go(lambda: copy(m.fix.at[0], m.fix.at[0], m.hop_send.at[4], m.fix_recv.at[0], 0), four)
        raise_fix(0)
        spread_tile(m.t_buf, m.t_send, m.t_recv)

        @pl.when(plane)
        def _():
            for step in range(1, 4):
                source = lax.rem(lvl + step, 4)
                arrived(m.fbuf.at[0, source], m.f_recv.at[0, source])

        @pl.when(four)
        def _():
            for k in range(4):
                arrived(m.fbuf.at[0, k], m.f_recv.at[0, k])

        correct(0, m.sol)

        halo_go(2, m.sol, SLOTS * B)

        image(2, m.sol, m.smooth)
        resid = m.field.at[3]
        resid[...] = m.rhs[...] - m.smooth[...]
        halo_go(3, resid, SLOTS * B, plane)
        terms = restrict(1, lambda s: m.field[3, pl.ds(s * B, B)])
        send_terms(1)
        for k in range(1, 4):
            go(
                lambda k=k: copy(m.rs_src.at[1, k], m.hop_in, m.four_send.at[4 + k], m.hop_recv, 4 + k),
                four,
            )
        @pl.when(plane)
        def _():
            for step in range(1, 4):
                source = lax.rem(lvl + step, 4)
                arrived(m.t_buf.at[source], m.t_recv.at[source])

        @pl.when(four)
        def _():
            for k in range(4):
                arrived(m.t_buf.at[k], m.t_recv.at[k])

        for k in range(4):
            m.t_part[k] = stacked(m.t_buf[k])

        total = jnp.zeros((B, B), F32)
        for s in range(SLOTS):
            total = total + product(m.t_part[targets[0, 0, 0, s]], beside(terms[s]))
        m.u_src[...] = total
        slot = jnp.maximum(lvl - 1, 0)
        go(
            lambda: copy(m.u_src, m.u_in.at[slot], m.u_send, m.u_recv.at[slot], 0),
            jnp.logical_not(root),
        )
        go(
            lambda: copy(m.rs_src.at[1, 0], m.rs_in.at[1, 4], m.four_send.at[4], m.rs_recv.at[1, 4], 0),
            four,
        )
        halo_go(3, resid, SLOTS * B, four)

        mid_sides = (m.mv, m.mhalo, m.mhalo_send, m.mhalo_recv)
        top_sides = (m.kv, m.khalo, m.khalo_send, m.khalo_recv)

        def mid_image(turn):
            return side_image(turn, lambda d: m.small[0, d], m.mv, m.mhalo, m.mhalo_recv)

        def top_image(turn):
            return side_image(turn, lambda d: m.small[1, d], m.kv, m.khalo, m.khalo_recv)

        @pl.when(plane)
        def _():
            total = plane_sum(1)
            arrived(m.rs_in.at[1, 4], m.rs_recv.at[1, 4])
            m.mv[0] = total + m.rs_in[1, 4]

        side_go(0, *mid_sides, plane)

        @pl.when(root)
        def _():
            total = m.u_src[...]
            for i in range(4):
                arrived(m.u_in.at[i], m.u_recv.at[i])
                total = total + m.u_in[i]
            m.kv[0] = total

        side_go(0, *top_sides, root)

        @pl.when(plane)
        def _():
            arrived(m.a_buf, m.a_recv)
            for d in range(3):
                m.small[0, d] = stacked(m.a_buf[d])

        @pl.when(root)
        def _():
            arrived(m.ac, m.ac_recv)
            for d in range(3):
                m.small[1, d] = stacked(m.ac[d])

        first = m.field.at[4]
        image(3, resid, first)

        @pl.when(plane)
        def _():
            m.mv[1] = mid_image(0)

        side_go(1, *mid_sides, plane)

        @pl.when(root)
        def _():
            m.kv[1] = top_image(0)

        side_go(1, *top_sides, root)
        halo_go(4, first, SLOTS * B)

        @pl.when(plane)
        def _():
            m.fbuf[1, lvl] = COEF_ZERO * m.mv[0] + COEF_ONE * m.mv[1] + COEF_TWO * mid_image(1)

        gather_go(1)
        go(
            lambda: copy(m.fbuf.at[1, lvl], m.fbuf.at[1, lvl], m.f_send.at[0, 0], m.f_recv.at[1, lvl], 4),
            plane,
        )
        go(
            lambda: copy(
                m.fbuf.at[1, lvl], m.mid_out.at[lax.rem(lvl, 2)], m.mid_send, m.mid_out_recv.at[lax.rem(lvl, 2)],
                5 + lvl // 2,
            ),
            plane & jnp.logical_not(root),
        )
        @pl.when(root)
        def _():
            m.fix[1] = COEF_ZERO * m.kv[0] + COEF_ONE * m.kv[1] + COEF_TWO * top_image(1)

        for to in (4, 2, 1, 3):
            go(
                lambda to=to: copy(
                    m.fix.at[1], m.fix.at[1], m.fix_send.at[1, to], m.fix_recv.at[1], to
                ),
                root,
            )

        image(4, first, m.smooth)
        m.smooth[...] = m.sol[...] + blend(resid, first)

        @pl.when(four)
        def _():
            arrived(m.fbuf.at[1, 0], m.f_recv.at[1, 0])

        go(lambda: copy(m.fbuf.at[1, 0], m.mid_out.at[0], m.mid_send, m.mid_out_recv.at[0], 5), four)

        @pl.when(jnp.logical_not(root))
        def _():
            arrived(m.fix.at[1], m.fix_recv.at[1])

        go(
            lambda: copy(m.fix.at[1], m.fix.at[1], m.fix_send.at[1, 5], m.fix_recv.at[1], lvl + 4),
            plane & jnp.logical_not(root),
        )
        raise_fix(1)

        @pl.when(plane)
        def _():
            for step in range(1, 4):
                source = lax.rem(lvl + step, 4)
                arrived(m.fbuf.at[1, source], m.f_recv.at[1, source])

        @pl.when(four)
        def _():
            for k in range(1, 4):
                arrived(m.fbuf.at[1, k], m.f_recv.at[1, k])

        correct(1, m.res)
        drain()
        for slot in range(SLOTS):
            stored(slot)

    def hop_up():
        arrived(m.hop_in, m.hop_recv)
        go(lambda: copy(m.hop_in, m.rs_in.at[1, 4], m.hop_send.at[1], m.rs_recv.at[1, 4], lvl - 4))

    @pl.when(is_mid)
    def _():
        pair = lvl - 5
        m.res[pl.ds(B, B)] = jnp.zeros((B, B), F32)
        store(m.res.at[pl.ds(B, B)], 1)
        load_links.wait()
        eye = (
            lax.broadcasted_iota(jnp.int32, (B, B), 0) == lax.broadcasted_iota(jnp.int32, (B, B), 1)
        ).astype(F32)
        for p in range(2):
            tile = m.links[2 * p, 0] + 0.5 * eye
            m.t_src[p] = tile
            m.link_parts[2 * p, 0] = stacked(tile)
            m.link_parts[2 * p, 1] = stacked(m.links[2 * p, 1])
        load_rhs.wait()
        meet()
        def smooth_go(p, way, to):
            k = 2 * pair + p
            go(lambda: copy(m.fbuf.at[0, k], m.fbuf.at[0, k], m.f_send.at[p, way], m.f_recv.at[0, k], to))

        def ship(src, dst, recv, send, k):
            go(lambda: copy(src, dst, send.at[0], recv, 4))
            go(lambda: copy(src, dst, send.at[1], recv, k), k > 0)

        for p in range(2):
            k = 2 * pair + p
            ship(m.links.at[2 * p, 1], m.p_buf.at[k], m.p_recv.at[k], m.p_send.at[pl.ds(2 * p, 2)], k)
        load_ops.wait()
        for p in range(2):
            for d in range(3):
                tile = gathered_tile(2 * p, d * SLOTS + 2 * p)
                m.a_src[p, d] = tile
                m.small[p, d] = stacked(tile)
        for p in range(2):
            k = 2 * pair + p
            to = k + 4 * (1 - (lax.rem(k, 3) + 1) // 2)
            go(lambda p=p, to=to: copy(m.a_src.at[p], m.a_buf, m.a_send.at[p], m.a_recv, to))
        for p in range(2):
            k = 2 * pair + p
            go(
                lambda p=p, k=k: copy(
                    m.t_src.at[p], m.t_buf.at[k], m.t_send.at[p], m.t_recv.at[k], k
                )
            )

        def level_image(turn, dst):
            for p in range(2):
                part = pl.ds(p * B, B)
                dst[part] = product(m.small[p, 1], beside(m.field[turn, part]))
            for side in range(2):
                @pl.when(has[side])
                def _():
                    halo_arrived(turn, side, 2 * B)
                    for p in range(2):
                        part = pl.ds(p * B, B)
                        dst[part] = dst[part] + product(
                            m.small[p, 2 * side], beside(m.halo[turn, side, part])
                        )

        for p in range(2):
            for source in (1, 0):
                arrived(m.mid_in.at[p, source], m.mid_recv.at[p, source])
            m.field[0, pl.ds(p * B, B)] = m.mid_in[p, 0] + m.mid_in[p, 1]
        total = product(m.link_parts[0, 0], beside(m.field[0, pl.ds(0, B)]))
        m.part_src[...] = total + product(m.link_parts[2, 0], beside(m.field[0, pl.ds(B, B)]))
        go(lambda: copy(m.part_src, m.coarse_in.at[pair], m.part_send, m.coarse_recv.at[pair], 7))
        halo_go(0, m.field.at[0], 2 * B)
        level_image(0, m.field.at[1])
        halo_go(1, m.field.at[1], 2 * B)
        level_image(1, m.smooth)
        part = pl.ds(0, 2 * B)
        m.smooth[part] = (
            COEF_ZERO * m.field[0, part] + COEF_ONE * m.field[1, part] + COEF_TWO * m.smooth[part]
        )
        for p in range(2):
            k = 2 * pair + p
            m.fbuf[0, k] = m.smooth[pl.ds(p * B, B)]
        for q in range(2):
            p = lax.rem(q + pair, 2)
            smooth_go(p, 0, 2 * pair + p)
        for p in range(2):
            smooth_go(p, 1, 4)
        arrived(m.fix.at[0], m.fix_recv.at[0])
        go(lambda: copy(m.fix.at[0], m.fix.at[0], m.hop_send.at[0], m.fix_recv.at[0], lvl - 4))
        for p in range(2):
            k = 2 * pair + p
            go(lambda p=p, k=k: copy(m.t_src.at[p], m.t_buf.at[k], m.t_send.at[2 + p], m.t_recv.at[k], 4))
        hop_up()
        arrived(m.fix.at[1], m.fix_recv.at[1])
        for p in range(2):
            m.lift[p] = product(m.link_parts[2 * p, 1], beside(m.fix[1]))
        for p in range(2):
            arrived(m.mid_out.at[p], m.mid_out_recv.at[p])
            rows = pl.ds(2 * p * B, B)
            m.res[rows] = m.mid_out[p] + m.lift[p]
            store(m.res.at[rows], 2 * p)
        drain()
        for slot in range(SLOTS):
            stored(slot)

    @pl.when(is_coarse)
    def _():
        m.res[...] = jnp.zeros((SLOTS * B, B), F32)
        for slot in (0, 2):
            store(m.res.at[pl.ds(slot * B, B)], slot)
        load_links.wait()
        load_rhs.wait()
        load_ops.wait()
        for d in range(3):
            m.ac[d] = gathered_tile(1, d * SLOTS + 1)
        clear_missing(m.chalo, has_far)
        meet()
        for side in range(2):
            go(
                lambda side=side: copy(
                    m.ac, m.ahalo.at[1 - side], m.ahalo_send.at[side], m.ahalo_recv.at[1 - side], lvl, near[side]
                ),
                has[side],
            )
        go(lambda: copy(m.ac, m.ac, m.st_send, m.ac_recv, 0))
        eye = (
            lax.broadcasted_iota(jnp.int32, (B, B), 0) == lax.broadcasted_iota(jnp.int32, (B, B), 1)
        ).astype(F32)
        centre = stacked(m.ac[1])
        m.st[0] = jnp.zeros((B, B), F32)
        m.st[1] = COEF_ONE * m.ac[0] + COEF_TWO * product(centre, beside(m.ac[0]))
        m.st[2] = COEF_ZERO * eye + COEF_ONE * m.ac[1] + COEF_TWO * product(centre, beside(m.ac[1]))
        m.st[3] = COEF_ONE * m.ac[2] + COEF_TWO * product(centre, beside(m.ac[2]))
        m.st[4] = jnp.zeros((B, B), F32)
        for side in range(2):
            @pl.when(has[side])
            def _():
                arrived(m.ahalo.at[side], m.ahalo_recv.at[side])
                edge = stacked(m.ac[2 * side])
                for d in range(3):
                    to = 2 * side + d
                    m.st[to] = m.st[to] + COEF_TWO * product(edge, beside(m.ahalo[side, d]))
        st_own = stacked(m.st[2])
        for i, d in enumerate((0, 1, 3, 4)):
            m.st_far[:, pl.ds(i * B, B)] = stacked(m.st[d])
        for pair in range(2):
            arrived(m.coarse_in.at[pair], m.coarse_recv.at[pair])
        m.cv[...] = m.coarse_in[0] + m.coarse_in[1]
        for i in range(4):
            go(
                lambda i=i: copy(
                    m.cv, m.chalo.at[3 - i], m.chalo_send.at[i], m.chalo_recv.at[3 - i], lvl, row + far[i]
                ),
                has_far[i],
            )
        own = product(st_own, beside(m.cv[...]))
        for i in range(4):
            @pl.when(has_far[i])
            def _():
                arrived(m.chalo.at[i], m.chalo_recv.at[i])
        m.fix[0] = own + product(m.st_far[...], beside(m.chalo[...].reshape(4 * B, B)))
        for to in (5, 4, 6, 3):
            go(
                lambda to=to: copy(
                    m.fix.at[0], m.fix.at[0], m.fix_send.at[0, to], m.fix_recv.at[0], to
                )
            )
        arrived(m.a_buf, m.a_recv)
        go(lambda: copy(m.a_buf, m.a_buf, m.a_send.at[0], m.a_recv, 3))
        hop_up()
        arrived(m.fix.at[1], m.fix_recv.at[1])
        store(m.fix.at[1], 1)
        drain()
        for slot in range(SLOTS):
            stored(slot)


def scratch():
    dma = lambda *shape: pltpu.SemaphoreType.DMA(shape)
    block = lambda *lead: pltpu.VMEM(lead + (B, B), F32)
    slab = lambda *lead: pltpu.VMEM(lead + (SLOTS * B, B), F32)
    parts = lambda *lead: pltpu.VMEM(lead + (2 * B, B), BF16)
    return dict(
        rhs=slab(), ops=block(SLOTS * OPT), links=block(SLOTS, 2),
        wide=pltpu.VMEM((3, 2 * SLOTS * B, SLOTS * B), BF16), small=parts(2, 3), link_parts=parts(SLOTS, 2),
        field=slab(5), halo=slab(5, 2), sol=slab(), smooth=slab(),
        rs_src=block(2, 4), rs_in=block(2, 5), sum_src=block(), mid_in=block(2, 2),
        part_src=block(), coarse_in=block(2), fix=block(2), fbuf=block(2, 4),
        t_src=block(2), t_buf=block(4), t_part=parts(4), p_buf=block(4), p_part=parts(4), lift=block(SLOTS), hop_in=block(), res=slab(),
        a_src=block(2, 3), a_buf=block(3), ac=block(3), ahalo=block(2, 3),
        st=block(5), st_far=pltpu.VMEM((2 * B, 4 * B), BF16),
        cv=block(), chalo=block(4), kv=block(2), khalo=block(2, 2), u_src=block(), u_in=block(4),
        mv=block(2), mhalo=block(2, 2), mid_out=block(2),
        in_sem=dma(3), out_sem=dma(SLOTS), halo_send=dma(5, 2), halo_recv=dma(5, 2),
        rs_send=dma(2, 4), rs_recv=dma(2, 5), sum_send=pltpu.SemaphoreType.DMA, mid_recv=dma(2, 2),
        four_send=dma(8), part_send=pltpu.SemaphoreType.DMA, coarse_recv=dma(2),
        fix_send=dma(2, 8), fix_recv=dma(2), f_send=dma(2, 2), gather_send=dma(2, 4), f_recv=dma(2, 4),
        t_send=dma(4), t_recv=dma(4), p_send=dma(4), p_recv=dma(4), hop_send=dma(5), hop_recv=pltpu.SemaphoreType.DMA,
        a_send=dma(2), a_recv=pltpu.SemaphoreType.DMA, ahalo_send=dma(2), ahalo_recv=dma(2),
        st_send=pltpu.SemaphoreType.DMA, ac_recv=pltpu.SemaphoreType.DMA,
        chalo_send=dma(4), chalo_recv=dma(4), khalo_send=dma(2, 2), khalo_recv=dma(2, 2), u_send=pltpu.SemaphoreType.DMA, u_recv=dma(4),
        mhalo_send=dma(2, 2), mhalo_recv=dma(2, 2), mid_send=pltpu.SemaphoreType.DMA, mid_out_recv=dma(2),
    )


def solution(mesh):
    n_row = mesh.shape["row"]

    def per_device(rhs, op_tiles, op_cols, link_tiles, level_links):
        held = scratch()
        out = pl.pallas_call(
            functools.partial(kernel, n_row, tuple(held)),
            name="multigrid",
            out_shape=jax.ShapeDtypeStruct((SLOTS * B, B), F32),
            in_specs=[
                pl.BlockSpec(memory_space=pl.ANY),
                pl.BlockSpec(memory_space=pl.ANY),
                pl.BlockSpec(memory_space=pltpu.SMEM),
                pl.BlockSpec(memory_space=pl.ANY),
                pl.BlockSpec(memory_space=pltpu.SMEM),
            ],
            out_specs=pl.BlockSpec(memory_space=pl.ANY),
            scratch_shapes=list(held.values()),
            compiler_params=pltpu.CompilerParams(
                collective_id=0, has_side_effects=True, vmem_limit_bytes=60 * 1024 * 1024
            ),
        )(
            rhs.reshape(SLOTS * B, B),
            op_tiles.reshape(SLOTS * OPT, B, B),
            op_cols.transpose(0, 2, 1, 3),
            link_tiles.reshape(SLOTS, 2, B, B),
            level_links.transpose(0, 1, 3, 2),
        )
        return out.reshape(1, 1, SLOTS, B, B)

    placed = (
        P("lvl", "row", None, None, None),
        P("lvl", "row", None, None, None, None),
        P("lvl", "row", None, None),
        P("lvl", "row", None, None, None, None),
        P("lvl", "row", None, None),
    )
    return jax.shard_map(
        per_device,
        mesh=mesh,
        in_specs=placed,
        out_specs=P("lvl", "row", None, None, None),
        check_vma=False,
    )
```
